32 devices in a mesh: dp: 4 (over z), fsdp: 8 (over y, x, core).
Axes of the slice: x: 2, y: 2, z: 4, core: 2. Of those that a mesh axis runs over, the one named last changes fastest.
Arguments:
- block_input: bfloat16 [8192, 768], P(('dp', 'fsdp')), may hold values from -6 to 6
- segment_ids: int32 [32, 256], P(('dp', 'fsdp')), may hold values from 0 to 7, never falling along the last dimension, each value on 1 to 128 neighbouring positions
- output_grad: bfloat16 [8192, 768], P(('dp', 'fsdp')), may hold values from -6 to 6
- prenorm_one: bfloat16 [768], P(('dp', 'fsdp')), may hold values from 0.25 to 1.75
- inproj_one: bfloat16 [768, 2304], P(('dp', 'fsdp')), may hold values from -0.21875 to 0.21875
- outproj_one: bfloat16 [768, 768], P(None, ('dp', 'fsdp')), may hold values from -0.875 to 0.875
- midnorm_one: bfloat16 [768], P(('dp', 'fsdp')), may hold values from 0.25 to 1.75
- expand_one: bfloat16 [768, 3072], P(('dp', 'fsdp')), may hold values from -0.21875 to 0.21875
- shrink_one: bfloat16 [3072, 768], P(None, ('dp', 'fsdp')), may hold values from -0.21875 to 0.21875
- prenorm_two: bfloat16 [768], P(('dp', 'fsdp')), may hold values from 0.25 to 1.75
- inproj_two: bfloat16 [768, 1920], P(('dp', 'fsdp')), may hold values from -0.21875 to 0.21875
- outproj_two: bfloat16 [768, 768], P(None, ('dp', 'fsdp')), may hold values from -0.875 to 0.875
- midnorm_two: bfloat16 [768], P(('dp', 'fsdp')), may hold values from 0.25 to 1.75
- expand_two: bfloat16 [768, 3072], P(('dp', 'fsdp')), may hold values from -0.21875 to 0.21875
- shrink_two: bfloat16 [3072, 768], P(None, ('dp', 'fsdp')), may hold values from -0.21875 to 0.21875
Outputs:
- block_output: float32 [8192, 768], P(('dp', 'fsdp'))
- input_grad: float32 [8192, 768], P(('dp', 'fsdp'))
- prenorm_one_grad: float32 [768], P(('dp', 'fsdp'))
- inproj_one_grad: float32 [768, 2304], P(('dp', 'fsdp'))
- outproj_one_grad: float32 [768, 768], P(None, ('dp', 'fsdp'))
- midnorm_one_grad: float32 [768], P(('dp', 'fsdp'))
- expand_one_grad: float32 [768, 3072], P(('dp', 'fsdp'))
- shrink_one_grad: float32 [3072, 768], P(None, ('dp', 'fsdp'))
- prenorm_two_grad: float32 [768], P(('dp', 'fsdp'))
- inproj_two_grad: float32 [768, 1920], P(('dp', 'fsdp'))
- outproj_two_grad: float32 [768, 768], P(None, ('dp', 'fsdp'))
- midnorm_two_grad: float32 [768], P(('dp', 'fsdp'))
- expand_two_grad: float32 [768, 3072], P(('dp', 'fsdp'))
- shrink_two_grad: float32 [3072, 768], P(None, ('dp', 'fsdp'))
The draws below stay inside these ranges and needn't reach their ends.
Inputs may be any that keep to these rules, and one draw needn't show every extreme that they name: `segment_ids`: within each row the numbers never fall; each document has 1 to 128 tokens, and one has exactly 128.
All inputs are finite; a program needn't handle non-finite values.
Results may differ from the reference program's by a relative error of at most 0.019.
Values may be sent and summed in bfloat16 or wider, within the bound.
A program may use at most 256 MiB of HBM per device.

```python
import math
import jax
import jax.numpy as jnp
import numpy as np
from jax import lax

D = 768
HEADS = 12
FF = 3072
TOK_DEV = 256
DOCS = 8
ROWS = 32
TOKENS = 8192
N_DP = 4
N_FSDP = 8


def raised(drawn, own_key, source, target, blocks, factor):
    owner, partner = [(jnp.arange(drawn.shape[position]) // (drawn.shape[position] // blocks)).reshape([-1 if axis == position else 1 for axis in range(drawn.ndim)]) for position in (source, target)]
    chosen = jax.random.permutation(own_key, blocks)[partner]
    strong = (owner == chosen) | (owner == (partner + blocks // 2) % blocks)
    return jnp.where(strong, factor * drawn, drawn)


def levels(own_key, shape, pieces, least, high):
    level = 1.0
    for dim, parts in pieces:
        steps = jax.random.uniform(jax.random.fold_in(jax.random.fold_in(own_key, 6), dim), (parts,), jnp.float32, least / len(pieces), high / len(pieces))
        level = level * jnp.repeat(jnp.exp(steps), shape[dim] // parts).reshape((-1,) + (1,) * (len(shape) - 1 - dim))
    return level


def profile(count, total, reach, lean):
    loads = [(1 << 20) // math.isqrt(standing ** lean) + 1 for standing in range(2, count + 1)]
    rest, counts = total - reach - (count - 1), [1] * (count - 1)
    while rest > 0:
        movable = [i for i in range(count - 1) if counts[i] < reach]
        mass, left = sum([loads[i] for i in movable]), rest
        for i in movable:
            more = min(reach - counts[i], max(1, left * loads[i] // mass), rest)
            counts[i] = counts[i] + more
            rest = rest - more
    return np.array([reach] + counts)


def uneven(rng, amount, total, limit, slope):
    if amount == 2:
        one = jax.random.randint(rng, (), max(1, total - limit), min(limit, total - 1) + 1)
        return jnp.stack([one, total - one])
    lengths = jnp.asarray(profile(amount, total, limit, slope), jnp.int32)
    couples = (amount - 1) // 2
    donor, taker = lengths[1:1 + 2 * couples:2], lengths[2:2 + 2 * couples:2]
    margin = jnp.minimum(donor - 1, limit - taker)
    shifted = jax.random.randint(jax.random.fold_in(rng, 1), (couples,), 0, 1 << 20) % (margin + 1)
    lengths = lengths.at[1:1 + 2 * couples:2].set(donor - shifted).at[2:2 + 2 * couples:2].set(taker + shifted)
    return lengths[jax.random.permutation(jax.random.fold_in(rng, 2), amount)]


def noise(stream_key, extent, scale, most, split=(), kind=jnp.bfloat16):
    values = scale * jax.random.normal(stream_key, extent, jnp.float32)
    if split:
        values = values * levels(stream_key, extent, split, -0.22, 0.18)
    return jnp.clip(values, -most, most).astype(kind)


def gaussian_with(own_key, dims, scale, limit, cuts, heavy, dtype=jnp.bfloat16):
    array = scale * jax.random.normal(own_key, dims, jnp.float32)
    if cuts:
        array = array * levels(own_key, dims, cuts, -0.22, 0.18)
    return jnp.clip(raised(array, jax.random.fold_in(own_key, 3), *heavy), -limit, limit).astype(dtype)


def setup_inputs(seed: int = 0) -> dict:
    key_of = jax.random.split(jax.random.key(seed), 16)
    return {
        "block_input": noise(key_of[0], (TOKENS, D), 1.0, 6.0, ((0, 32),)),
        "segment_ids": jax.vmap(lambda own: jnp.searchsorted(jnp.cumsum(uneven(own, DOCS, TOK_DEV, TOK_DEV // 2, 2)), jnp.arange(TOK_DEV), side="right"))(jax.random.split(key_of[1], ROWS)).reshape((ROWS, TOK_DEV)).astype(jnp.int32),
        "output_grad": gaussian_with(key_of[2], (TOKENS, D), 1.0, 6.0, ((0, 32),), (0, 1, 32, 2.75)),
        "prenorm_one": jnp.clip(1.0 + 0.15 * jax.random.normal(key_of[3], (D,), jnp.float32), 0.25, 1.75).astype(jnp.bfloat16),
        "inproj_one": noise(key_of[4], (D, 3 * D), D ** -0.5, 0.21875, ((0, 32),)),
        "outproj_one": noise(key_of[5], (D, D), (D // 16) ** -0.5, 0.875, ((1, 32),)),
        "midnorm_one": jnp.clip(1.0 + 0.15 * jax.random.normal(key_of[6], (D,), jnp.float32), 0.25, 1.75).astype(jnp.bfloat16),
        "expand_one": noise(key_of[7], (D, FF), D ** -0.5, 0.21875, ((0, 32),)),
        "shrink_one": noise(key_of[8], (FF, D), (FF // 4) ** -0.5, 0.21875, ((1, 32),)),
        "prenorm_two": jnp.clip(1.0 + 0.15 * jax.random.normal(key_of[9], (D,), jnp.float32), 0.25, 1.75).astype(jnp.bfloat16),
        "inproj_two": noise(key_of[10], (D, 5 * D // 2), D ** -0.5, 0.21875, ((0, 32),)),
        "outproj_two": noise(key_of[11], (D, D), (D // 16) ** -0.5, 0.875, ((1, 32),)),
        "midnorm_two": jnp.clip(1.0 + 0.15 * jax.random.normal(key_of[12], (D,), jnp.float32), 0.25, 1.75).astype(jnp.bfloat16),
        "expand_two": noise(key_of[13], (D, FF), D ** -0.5, 0.21875, ((0, 32),)),
        "shrink_two": noise(key_of[14], (FF, D), (FF // 4) ** -0.5, 0.21875, ((1, 32),)),
    }


@jax.custom_vjp
def low(v):
    return lax.optimization_barrier(v.astype(jnp.bfloat16)).astype(jnp.float32)

@jax.custom_vjp
def low_back(v):
    return v

def low_keep(v):
    return (low(v), None)

def low_pass(kept, grad):
    return (grad,)

def back_keep(v):
    return (v, None)

def back_low(kept, grad):
    return (low(grad),)
low.defvjp(low_keep, low_pass)
low_back.defvjp(back_keep, back_low)

def product(left, right):
    return jnp.dot(left, right, precision=lax.Precision.HIGHEST, preferred_element_type=jnp.float32)

def layer_norm(inputs, gain):
    centred = inputs - lax.optimization_barrier(jnp.mean(inputs, axis=-1, keepdims=True))
    spread = lax.optimization_barrier(jnp.mean(centred * centred, axis=-1, keepdims=True))
    return centred * lax.rsqrt(spread + 1e-05) * gain

def attend(query, keys, values, segment):
    groups, length = segment.shape
    width = query.shape[-1]
    size = width // HEADS
    scale = 1.0 / math.sqrt(size)
    query_heads = query.reshape(groups, length, HEADS, size)
    key_heads = keys.reshape(groups, length, HEADS, size)
    value_heads = values.reshape(groups, length, HEADS, size)
    scores = jnp.einsum('gqhd,gkhd->ghqk', query_heads, key_heads, precision=lax.Precision.HIGHEST) * scale
    scores = low_back(scores)
    positions = jnp.arange(length)
    allowed = (segment[:, :, None] == segment[:, None, :]) & (positions[None, None, :] <= positions[None, :, None])
    scores = jnp.where(allowed[:, None], scores, -1000000000.0)
    highest = lax.optimization_barrier(jnp.max(scores, axis=-1, keepdims=True))
    total = highest + jnp.log(lax.optimization_barrier(jnp.sum(jnp.exp(scores - highest), axis=-1, keepdims=True)))
    probs = low(jnp.exp(scores - total))
    mixed = jnp.einsum('ghqk,gkhd->gqhd', probs, value_heads, precision=lax.Precision.HIGHEST)
    return low(low_back(mixed.reshape(groups * length, width)))

def layer(inputs, segment, weights, first_values):
    prenorm, inproj, outproj, midnorm, expand, shrink = weights
    width = inputs.shape[-1]
    half = width // 2
    attn_in = low(layer_norm(inputs, prenorm))
    projected = product(attn_in, inproj)
    query = low(low_back(projected[:, :width]))
    keys = low(low_back(projected[:, width:2 * width]))
    fresh = low(low_back(projected[:, 2 * width:]))
    if first_values is None:
        values = fresh
    else:
        values = jnp.concatenate([first_values[:, :half], fresh], axis=1)
    mixed = attend(query, keys, values, segment)
    middle = inputs + low_back(product(mixed, outproj))
    mlp_in = low(layer_norm(middle, midnorm))
    before = low_back(product(mlp_in, expand))
    active = low(jax.nn.gelu(before, approximate=True))
    return (middle + low_back(product(active, shrink)), fresh)

def block(inputs, segment, first_weights, second_weights):
    hidden, first_values = layer(inputs, segment, first_weights, None)
    output, unused = layer(hidden, segment, second_weights, first_values)
    return output

def reference(block_input, segment_ids, output_grad, prenorm_one, inproj_one, outproj_one, midnorm_one, expand_one, shrink_one, prenorm_two, inproj_two, outproj_two, midnorm_two, expand_two, shrink_two):
    count = N_DP * N_FSDP
    group = 1
    while group * 2 * TOK_DEV <= 4096 and count % (group * 2) == 0:
        group = group * 2
    blocks = count // group
    inputs = block_input.astype(jnp.float32).reshape(blocks, group * TOK_DEV, D)
    segments = segment_ids.reshape(blocks, group, TOK_DEV)
    first_weights = tuple((w.astype(jnp.float32) for w in (prenorm_one, inproj_one, outproj_one, midnorm_one, expand_one, shrink_one)))
    second_weights = tuple((w.astype(jnp.float32) for w in (prenorm_two, inproj_two, outproj_two, midnorm_two, expand_two, shrink_two)))
    checked = jax.checkpoint(block)

    def whole(values, weights_a, weights_b):
        return lax.map(lambda pair: checked(pair[0], pair[1], weights_a, weights_b), (values, segments))
    output, pullback = jax.vjp(whole, inputs, first_weights, second_weights)
    cotangent = output_grad.astype(jnp.float32).reshape(blocks, group * TOK_DEV, D)
    input_grad, grads_a, grads_b = pullback(cotangent)
    return (output.reshape(TOKENS, D), input_grad.reshape(TOKENS, D), grads_a[0], grads_a[1], grads_a[2], grads_a[3], grads_a[4], grads_a[5], grads_b[0], grads_b[1], grads_b[2], grads_b[3], grads_b[4], grads_b[5])
```

```python
import functools
import math

import jax
import jax.numpy as jnp
from jax import lax
from jax.experimental import pallas as pl
from jax.experimental.pallas import tpu as pltpu
from jax.sharding import PartitionSpec as P

HEADS = 12


def layer_norm(inputs, gain):
    centred = inputs - jnp.mean(inputs, axis=-1, keepdims=True)
    spread = jnp.mean(centred * centred, axis=-1, keepdims=True)
    return centred * lax.rsqrt(spread + 1e-05) * gain


def gelu_tanh(value):
    return jax.nn.gelu(value, approximate=True)


def rows_product(left, right):
    return lax.dot_general(
        left, right, (((0,), (0,)), ((), ())), preferred_element_type=jnp.float32
    )


def cols_product(left, right):
    return lax.dot_general(
        left, right, (((1,), (1,)), ((), ())), preferred_element_type=jnp.float32
    )


def gather_weights(weights):
    prenorm, inproj, outproj, midnorm, expand, shrink = weights
    return (
        lax.all_gather(prenorm, ("dp", "fsdp"), axis=0, tiled=True),
        lax.all_gather(inproj, ("dp", "fsdp"), axis=0, tiled=True),
        lax.all_gather(outproj, ("dp", "fsdp"), axis=1, tiled=True),
        lax.all_gather(midnorm, ("dp", "fsdp"), axis=0, tiled=True),
        lax.all_gather(expand, ("dp", "fsdp"), axis=0, tiled=True),
        lax.all_gather(shrink, ("dp", "fsdp"), axis=1, tiled=True),
    )


def sum_grads(kept):
    (
        attn_in,
        proj_grad,
        branch_low,
        mixed,
        mlp_in,
        before_grad,
        out_low,
        active,
        prenorm_grad,
        midnorm_grad,
    ) = kept
    width = attn_in.shape[1]
    proj_width = proj_grad.shape[1]
    hidden_width = active.shape[1]

    def entries(value):
        return value[:, None]

    summed = lax.psum_scatter(
        jnp.concatenate(
            [
                rows_product(attn_in, proj_grad),
                rows_product(branch_low, mixed),
                rows_product(mlp_in, before_grad),
                rows_product(out_low, active),
                entries(prenorm_grad),
                entries(midnorm_grad),
            ],
            axis=1,
        ),
        ("dp", "fsdp"),
        scatter_dimension=0,
        tiled=True,
    )
    inproj_part = summed[:, :proj_width]
    outproj_part = summed[:, proj_width : proj_width + width].T
    expand_start = proj_width + width
    expand_part = summed[:, expand_start : expand_start + hidden_width]
    shrink_start = expand_start + hidden_width
    shrink_part = summed[:, shrink_start : shrink_start + hidden_width].T
    prenorm_part = summed[:, shrink_start + hidden_width]
    midnorm_part = summed[:, shrink_start + hidden_width + 1]
    return (prenorm_part, inproj_part, outproj_part, midnorm_part, expand_part, shrink_part)


def layer_forward(inputs, allowed, weights, first_values):
    prenorm, inproj, outproj, midnorm, expand, shrink = weights
    length, width = inputs.shape
    half = width // 2
    size = width // HEADS
    scale = 1.0 / math.sqrt(size)
    attn_in = layer_norm(inputs, prenorm.astype(jnp.float32)).astype(jnp.bfloat16)
    projected = jnp.dot(attn_in, inproj, preferred_element_type=jnp.float32)
    query = projected[:, :width].astype(jnp.bfloat16).reshape(length, HEADS, size)
    keys = projected[:, width : 2 * width].astype(jnp.bfloat16).reshape(length, HEADS, size)
    fresh = projected[:, 2 * width :].astype(jnp.bfloat16)
    if first_values is None:
        values = fresh
    else:
        values = jnp.concatenate([first_values[:, :half], fresh], axis=1)
    value_heads = values.reshape(length, HEADS, size)
    scores = jnp.einsum("qhd,khd->hqk", query, keys, preferred_element_type=jnp.float32) * scale
    scores = jnp.where(allowed[None], scores, -1000000000.0)
    highest = jnp.max(scores, axis=-1, keepdims=True)
    total = highest + jnp.log(jnp.sum(jnp.exp(scores - highest), axis=-1, keepdims=True))
    weights_full = jnp.exp(scores - total)
    probs = weights_full.astype(jnp.bfloat16)
    mixed = jnp.einsum("hqk,khd->qhd", probs, value_heads, preferred_element_type=jnp.float32)
    mixed = mixed.astype(jnp.bfloat16).reshape(length, width)
    middle = inputs + jnp.dot(mixed, outproj, preferred_element_type=jnp.float32)
    mlp_in = layer_norm(middle, midnorm.astype(jnp.float32)).astype(jnp.bfloat16)
    before = jnp.dot(mlp_in, expand, preferred_element_type=jnp.float32)
    active = gelu_tanh(before).astype(jnp.bfloat16)
    output = middle + jnp.dot(active, shrink, preferred_element_type=jnp.float32)
    return (
        attn_in,
        query,
        keys,
        fresh,
        value_heads,
        weights_full,
        probs,
        mixed,
        middle,
        mlp_in,
        before,
        active,
        output,
    )


def layer_backward(inputs, allowed, weights, first_values, incoming, carried, parts=None):
    prenorm, inproj, outproj, midnorm, expand, shrink = weights
    length, width = inputs.shape
    half = width // 2
    size = width // HEADS
    scale = 1.0 / math.sqrt(size)
    if parts is None:
        parts = layer_forward(inputs, allowed, weights, first_values)
    (
        attn_in,
        query,
        keys,
        fresh,
        value_heads,
        weights_full,
        probs,
        mixed,
        middle,
        mlp_in,
        before,
        active,
        output,
    ) = parts
    out_low = incoming.astype(jnp.bfloat16)
    active_grad = cols_product(out_low, shrink)
    unused_gelu, gelu_pull = jax.vjp(gelu_tanh, before)
    before_grad = gelu_pull(active_grad)[0].astype(jnp.bfloat16)
    mlp_grad = cols_product(before_grad, expand)
    unused_mid, mid_pull = jax.vjp(layer_norm, middle, midnorm.astype(jnp.float32))
    middle_part, midnorm_grad = mid_pull(mlp_grad)
    middle_grad = incoming + middle_part
    branch_low = middle_grad.astype(jnp.bfloat16)
    mixed_grad = cols_product(branch_low, outproj).astype(jnp.bfloat16).reshape(length, HEADS, size)
    prob_grad = jnp.einsum(
        "qhd,khd->hqk", mixed_grad, value_heads, preferred_element_type=jnp.float32
    )
    value_grad = jnp.einsum(
        "hqk,qhd->khd", probs, mixed_grad, preferred_element_type=jnp.float32
    ).reshape(length, width)
    score_grad = weights_full * (
        prob_grad - jnp.sum(weights_full * prob_grad, axis=-1, keepdims=True)
    )
    score_low = score_grad.astype(jnp.bfloat16)
    query_grad = (
        (jnp.einsum("hqk,khd->qhd", score_low, keys, preferred_element_type=jnp.float32) * scale)
        .astype(jnp.bfloat16)
        .reshape(length, width)
    )
    keys_grad = (
        (jnp.einsum("hqk,qhd->khd", score_low, query, preferred_element_type=jnp.float32) * scale)
        .astype(jnp.bfloat16)
        .reshape(length, width)
    )
    if first_values is None:
        value_total = jnp.concatenate(
            [value_grad[:, :half] + carried, value_grad[:, half:]], axis=1
        )
        fresh_grad = value_total.astype(jnp.bfloat16)
        passed = None
    else:
        fresh_grad = value_grad[:, half:].astype(jnp.bfloat16)
        passed = value_grad[:, :half]
    proj_grad = jnp.concatenate([query_grad, keys_grad, fresh_grad], axis=1)
    attn_grad = cols_product(proj_grad, inproj)
    unused_in, in_pull = jax.vjp(layer_norm, inputs, prenorm.astype(jnp.float32))
    inputs_part, prenorm_grad = in_pull(attn_grad)
    kept = (
        attn_in,
        proj_grad,
        branch_low,
        mixed,
        mlp_in,
        before_grad,
        out_low,
        active,
        prenorm_grad,
        midnorm_grad,
    )
    return (middle_grad + inputs_part, kept, passed)


PIECE = 384
CHUNK = 2 * PIECE
MESH = pl.DeviceIdType.MESH


def when(condition, body):
    if isinstance(condition, bool):
        if condition:
            body()
    else:
        pl.when(condition)(body)


class Seat:
    def __init__(self, layers):
        self.layers = layers
        self.z = lax.axis_index("dp")
        place = lax.axis_index("fsdp")
        self.core = lax.rem(place, 2)
        self.x = lax.rem(lax.div(place, 2), 2)
        self.y = lax.div(place, 4)
        self.partner = (self.z, place + 1 - 2 * self.core)
        self.across_x = (self.z, place + 2 - 4 * self.x)
        self.across_y = (self.z, place + 4 - 8 * self.y)
        self.up = (self.z + 1, place)
        self.down = (self.z - 1, place)
        self.has_up = self.z < layers - 1
        self.has_down = self.z > 0

    def greet(self):
        barrier = pltpu.get_barrier_semaphore()
        for other in (self.partner, self.across_x, self.across_y):
            pl.semaphore_signal(barrier, inc=1, device_id=other, device_id_type=MESH)

        @pl.when(self.has_up)
        def _():
            pl.semaphore_signal(barrier, inc=1, device_id=self.up, device_id_type=MESH)

        @pl.when(self.has_down)
        def _():
            pl.semaphore_signal(barrier, inc=1, device_id=self.down, device_id_type=MESH)

        inner = self.has_up & self.has_down

        @pl.when(inner)
        def _():
            pl.semaphore_wait(barrier, 5)

        @pl.when(jnp.logical_not(inner))
        def _():
            pl.semaphore_wait(barrier, 4)


def piece_columns(chunk, core):
    return pl.ds(pl.multiple_of(chunk * CHUNK + core * PIECE, 128), PIECE)


def remote(source, target, send_sem, recv_sem, device):
    return pltpu.make_async_remote_copy(
        src_ref=source,
        dst_ref=target,
        send_sem=send_sem,
        recv_sem=recv_sem,
        device_id=device,
        device_id_type=MESH,
    )


FULL = slice(None)
COLOURS = (0, 1, 2, 0, 1, 0, 1, 2)


def colour_of(chunk):
    step = lax.rem(chunk, 8)
    return jnp.where(
        (step == 2) | (step == 7), 2, jnp.where((step == 1) | (step == 4) | (step == 6), 1, 0)
    )


class Gather:
    def __init__(self, seat, held, own, other, chunks, pre_sem, recv_sem, send_sem):
        self.seat, self.held, self.own, self.other, self.chunks = seat, held, own, other, chunks
        self.pre_sem, self.recv_sem, self.send_sem = pre_sem, recv_sem, send_sem

    def window(self, chunk, zs, ys, xs, core=None):
        core = self.seat.core if core is None else core
        return self.held.at[zs, ys, xs, :, piece_columns(chunk, core)]

    def swap(self, chunk):
        seat = self.seat
        columns = piece_columns(chunk, 1 - seat.core)
        return remote(
            self.own.at[:, columns],
            self.other.at[:, columns],
            self.pre_sem.at[0, chunk],
            self.pre_sem.at[1, chunk],
            seat.partner,
        )

    def copy(self, chunk, zs, ys, xs, kind, arrival, device):
        window = self.window(chunk, zs, ys, xs)
        return remote(
            window, window, self.send_sem.at[chunk, kind], self.recv_sem.at[chunk, arrival], device
        )

    def up(self, chunk, origin, ys, xs):
        return self.copy(chunk, origin, ys, xs, origin, origin, self.seat.up)

    def down(self, chunk, origin, ys, xs):
        return self.copy(chunk, origin, ys, xs, 4 + origin, origin, self.seat.down)

    def merge(self, chunk):
        seat = self.seat
        columns = piece_columns(chunk, seat.core)
        remote(
            self.own.at[:, columns],
            self.other.at[:, columns],
            self.pre_sem.at[0, chunk],
            self.pre_sem.at[1, chunk],
            seat.partner,
        ).wait_recv()
        mine = self.own[:, columns].astype(jnp.float32)
        theirs = self.other[:, columns].astype(jnp.float32)
        first = seat.core == 0
        both = jnp.concatenate(
            [jnp.where(first, mine, theirs), jnp.where(first, theirs, mine)], axis=0
        )
        self.held[seat.z, seat.y, seat.x, :, columns] = both.astype(jnp.bfloat16)

    def start_z(self, chunk, ys, xs):
        seat = self.seat
        when(seat.has_up, lambda: self.up(chunk, seat.z, ys, xs).start())
        when(seat.has_down, lambda: self.down(chunk, seat.z, ys, xs).start())

    def relay_z(self, chunk, step, ys, xs):
        seat = self.seat
        below, above = seat.z - 1 - step, seat.z + 1 + step

        def from_below():
            self.up(chunk, below, ys, xs).wait_recv()
            when(seat.has_up, lambda: self.up(chunk, below, ys, xs).start())

        def from_above():
            self.down(chunk, above, ys, xs).wait_recv()
            when(seat.has_down, lambda: self.down(chunk, above, ys, xs).start())

        when(below >= 0, from_below)
        when(above <= seat.layers - 1, from_above)

    def side(self, chunk, axis, zs, other):
        seat = self.seat
        if axis == "x":
            return self.copy(chunk, zs, other, seat.x, 8, 4, seat.across_x)
        return self.copy(chunk, zs, seat.y, other, 9, 5, seat.across_y)

    def side_arrives(self, chunk, axis, zs, other):
        seat = self.seat
        if axis == "x":
            self.copy(chunk, zs, other, 1 - seat.x, 8, 4, seat.across_x).wait_recv()
        else:
            self.copy(chunk, zs, 1 - seat.y, other, 9, 5, seat.across_y).wait_recv()

    def to_partner(self, chunk):
        return self.copy(chunk, FULL, FULL, FULL, 10, 6, self.seat.partner)

    def stage(self, chunk, number):
        seat = self.seat
        y, x = seat.y, seat.x
        last = seat.layers - 1

        def z_first(first, second, own_first):
            if number == 0:
                self.start_z(chunk, y, x)
            elif number <= last:
                self.relay_z(chunk, number - 1, y, x)
            if number == last:
                self.side(chunk, first, FULL, own_first).start()
            if number == last + 1:
                self.side_arrives(chunk, first, FULL, own_first)
                self.side(chunk, second, FULL, FULL).start()
            if number == last + 2:
                self.side_arrives(chunk, second, FULL, FULL)

        def z_last():
            if number == 0:
                self.side(chunk, "x", seat.z, y).start()
            if number == 1:
                self.side_arrives(chunk, "x", seat.z, y)
                self.side(chunk, "y", seat.z, FULL).start()
            if number == 2:
                self.side_arrives(chunk, "y", seat.z, FULL)
                self.start_z(chunk, FULL, FULL)
            if number >= 3:
                self.relay_z(chunk, number - 3, FULL, FULL)

        if number == 0:
            self.merge(chunk)
        if number <= last + 2:
            colour = colour_of(chunk)
            when(colour == 0, lambda: z_first("x", "y", y))
            when(colour == 1, lambda: z_first("y", "x", x))
            when(colour == 2, z_last)
        if number == last + 2:
            self.to_partner(chunk).start()
        if number == last + 3:
            window = self.window(chunk, FULL, FULL, FULL, 1 - seat.core)
            remote(
                window, window, self.send_sem.at[chunk, 10], self.recv_sem.at[chunk, 6], seat.partner
            ).wait_recv()

    def drain(self, chunk):
        seat = self.seat
        y, x = seat.y, seat.x
        columns = piece_columns(chunk, 1 - seat.core)
        self.swap(chunk).wait_send()

        def z_sends(ys, xs):
            for origin in range(seat.layers):
                when(
                    seat.has_up & (seat.z >= origin),
                    lambda: self.up(chunk, origin, ys, xs).wait_send(),
                )
                when(
                    seat.has_down & (seat.z <= origin),
                    lambda: self.down(chunk, origin, ys, xs).wait_send(),
                )

        def z_first(first, second, own_first):
            z_sends(y, x)
            self.side(chunk, first, FULL, own_first).wait_send()
            self.side(chunk, second, FULL, FULL).wait_send()

        def z_last():
            z_sends(FULL, FULL)
            self.side(chunk, "x", seat.z, y).wait_send()
            self.side(chunk, "y", seat.z, FULL).wait_send()

        colour = colour_of(chunk)
        when(colour == 0, lambda: z_first("x", "y", y))
        when(colour == 1, lambda: z_first("y", "x", x))
        when(colour == 2, z_last)
        self.to_partner(chunk).wait_send()

    def round(self, i):
        for lag, number in ((0, 0), (2, 4), (1, 2), (3, 6), (2, 5), (1, 3), (0, 1)):
            chunk = i - lag
            when((chunk >= 0) & (chunk < self.chunks), functools.partial(self.stage, chunk, number))


def gather_kernel(layers, chunks, own, held, other, pre_sem, recv_sem, send_sem):
    seat = Seat(layers)
    seat.greet()
    work = Gather(seat, held, own, other, chunks, pre_sem, recv_sem, send_sem)

    def loop(count, body):
        lax.fori_loop(0, count, lambda i, c: (body(i), c)[1], 0)

    loop(chunks, lambda i: work.swap(i).start())
    loop(chunks + 3, work.round)
    loop(chunks, work.drain)


SLOTS = 6
LANDING = 23


class Scatter:
    def __init__(self, seat, chunks, fill, part, staged, landed, total, recv_sem, send_sem):
        self.seat, self.chunks, self.fill = seat, chunks, fill
        self.part, self.staged, self.landed, self.total = part, staged, landed, total
        self.recv_sem, self.send_sem = recv_sem, send_sem

    def send(self, turn, spot, there, count, kind, arrival, device):
        slot = lax.rem(turn, SLOTS)
        return remote(
            self.staged.at[slot, pl.ds(spot, count)],
            self.landed.at[turn, pl.ds(there, count)],
            self.send_sem.at[slot, kind],
            self.recv_sem.at[turn, arrival],
            device,
        )

    def store(self, turn, spot, count, zs, ys, xs):
        slot = lax.rem(turn, SLOTS)
        value = self.part[slot, zs, ys, xs]
        self.staged[slot, pl.ds(spot, count)] = value.astype(jnp.bfloat16).reshape(
            (count,) + value.shape[-2:]
        )

    def add(self, turn, spot, count, zs, ys, xs):
        slot = lax.rem(turn, SLOTS)
        value = self.part[slot, zs, ys, xs]
        arrived = self.landed[turn, pl.ds(spot, count)].astype(jnp.float32)
        self.part[slot, zs, ys, xs] = value + arrived.reshape(value.shape)

    def side(self, turn, axis, spot, count):
        device = self.seat.across_x if axis == "x" else self.seat.across_y
        kind = 0 if axis == "x" else 1
        return self.send(turn, spot, spot, count, kind, kind, device)

    def start_side(self, turn, axis, spot, count, zs, other):
        seat = self.seat
        if axis == "x":
            self.store(turn, spot, count, zs, other, 1 - seat.x)
        else:
            self.store(turn, spot, count, zs, 1 - seat.y, other)
        self.side(turn, axis, spot, count).start()

    def finish_side(self, turn, axis, spot, count, zs, other):
        seat = self.seat
        self.side(turn, axis, spot, count).wait_recv()
        if axis == "x":
            self.add(turn, spot, count, zs, other, seat.x)
        else:
            self.add(turn, spot, count, zs, seat.y, other)

    def up(self, turn, base, count, goal):
        return self.send(
            turn, base + count * goal, base + count * goal, count, 2 + goal, 2 + goal, self.seat.up
        )

    def down(self, turn, base, count, goal):
        slot = jnp.where(goal == self.seat.z - 1, self.seat.layers, goal)
        return self.send(
            turn, base + count * goal, base + count * slot, count, 2 + goal, 2 + slot, self.seat.down
        )

    def arrival_z(self, turn, base, count, slot):
        spot = pl.ds(base + count * slot, count)
        window = self.landed.at[turn, spot]
        return remote(
            window,
            window,
            self.send_sem.at[0, 0],
            self.recv_sem.at[turn, 2 + slot],
            self.seat.partner,
        )

    def step_z(self, turn, step, base, count, ys, xs):
        seat = self.seat
        layers = seat.layers

        def upward():
            for goal in range(1, layers):

                def one(goal=goal):
                    def arrived():
                        self.arrival_z(turn, base, count, goal).wait_recv()
                        self.add(turn, base + count * goal, count, goal, ys, xs)

                    when(seat.has_down, arrived)

                    def onward():
                        self.store(turn, base + count * goal, count, goal, ys, xs)
                        self.up(turn, base, count, goal).start()

                    when(seat.z < goal, onward)

                when(seat.z <= goal, one)

        def downward():
            for goal in range(layers - 1):

                def one(goal=goal):
                    def arrived():
                        slot = jnp.where(goal == seat.z, layers, goal)
                        self.arrival_z(turn, base, count, slot).wait_recv()
                        self.add(turn, base + count * slot, count, goal, ys, xs)

                    when(seat.has_up, arrived)

                    def onward():
                        self.store(turn, base + count * goal, count, goal, ys, xs)
                        self.down(turn, base, count, goal).start()

                    when(seat.z > goal, onward)

                when(seat.z >= goal, one)

        when(seat.z == step, upward)
        when(seat.z == layers - 1 - step, downward)

    def piece(self, turn):
        seat = self.seat
        slot = lax.rem(turn, SLOTS)
        rows = self.total.shape[0]
        return self.part.at[
            slot, seat.z, seat.y, seat.x, pl.ds(pl.multiple_of((1 - seat.core) * rows, 8), rows)
        ]

    def hand_over(self, turn, chunk):
        window = self.total.at[:, piece_columns(chunk, self.seat.core)]
        return remote(
            self.piece(turn),
            window,
            self.send_sem.at[lax.rem(turn, SLOTS), 6],
            self.recv_sem.at[turn, 7],
            self.seat.partner,
        )

    def stage(self, turn, number):
        seat = self.seat
        y, x, z = seat.y, seat.x, seat.z
        chunk = chunk_at(turn)

        def z_last(first, second, own_second):
            if number == 0:
                self.start_side(turn, first, 0, 8, FULL, FULL)
            if number == 1:
                self.finish_side(turn, first, 0, 8, FULL, FULL)
                self.start_side(turn, second, 8, 4, FULL, own_second)
            if number == 2:
                self.finish_side(turn, second, 8, 4, FULL, own_second)
            if 2 <= number <= 5:
                self.step_z(turn, number - 2, 12, 1, y, x)

        def z_first():
            if number <= 3:
                self.step_z(turn, number, 0, 4, FULL, FULL)
            if number == 3:
                self.start_side(turn, "y", 20, 2, z, FULL)
            if number == 4:
                self.finish_side(turn, "y", 20, 2, z, FULL)
                self.start_side(turn, "x", 22, 1, z, y)
            if number == 5:
                self.finish_side(turn, "x", 22, 1, z, y)

        if number == 0:
            self.fill(turn, chunk)
        if number <= 5:
            colour = colour_of(turn)
            when(colour == 0, lambda: z_last("y", "x", y))
            when(colour == 1, lambda: z_last("x", "y", x))
            when(colour == 2, z_first)
        if number == 5:
            slot = lax.rem(turn, SLOTS)
            rows = self.total.shape[0]
            mine = pl.ds(pl.multiple_of(seat.core * rows, 8), rows)
            self.total[:, piece_columns(chunk, seat.core)] = self.part[slot, z, y, x, mine]
            self.hand_over(turn, chunk).start()
        if number == 6:
            self.hand_over(turn, chunk).wait_send()
            window = self.total.at[:, piece_columns(chunk, 1 - seat.core)]
            remote(
                window, window, self.send_sem.at[0, 0], self.recv_sem.at[turn, 7], seat.partner
            ).wait_recv()
            self.drain(turn)

    def drain(self, turn):
        seat = self.seat

        def z_sends(base, count):
            for goal in range(seat.layers):
                when(seat.z < goal, lambda: self.up(turn, base, count, goal).wait_send())
                when(seat.z > goal, lambda: self.down(turn, base, count, goal).wait_send())

        def z_last(first, second):
            self.side(turn, first, 0, 8).wait_send()
            self.side(turn, second, 8, 4).wait_send()
            z_sends(12, 1)

        def z_first():
            z_sends(0, 4)
            self.side(turn, "y", 20, 2).wait_send()
            self.side(turn, "x", 22, 1).wait_send()

        colour = colour_of(turn)
        when(colour == 0, lambda: z_last("y", "x"))
        when(colour == 1, lambda: z_last("x", "y"))
        when(colour == 2, z_first)

    def round(self, i):
        for lag, number in ((0, 0), (2, 4), (1, 2), (3, 6), (2, 5), (1, 3), (0, 1)):
            turn = i - lag
            when((turn >= 0) & (turn < self.chunks), functools.partial(self.stage, turn, number))


def chunk_at(turn):
    spans = ((4, 20), (8, 12), (9, 7), (11, 4), (15, -2), (19, -10), (20, -15), (23, -19))
    chunk = turn - 23
    for end, shift in reversed(spans):
        if end == 4:
            chunk = jnp.where(turn < end, turn + shift, chunk)
        else:
            chunk = jnp.where(turn < end, turn + shift, chunk)
    return chunk


def left_of(chunk):
    kind = 4
    for start, which in ((1, 0), (4, 1), (5, 2), (9, 3), (13, 4), (15, 5), (16, 6), (20, 7)):
        kind = jnp.where(chunk >= start, which, kind)
    return kind


def scatter_kernel(
    layers,
    chunks,
    lefts,
    rights,
    gains,
    total,
    left2,
    right2,
    gain2,
    part,
    staged,
    landed,
    pre_sem,
    recv_sem,
    send_sem,
):
    seat = Seat(layers)
    seat.greet()
    core = seat.core
    moves = []
    for i, (source, target) in enumerate(
        ((lefts, left2), (rights, right2), (gains, gain2))
    ):
        moves.append(
            pltpu.make_async_copy(source, target.at[core], pre_sem.at[3 * i])
        )
        moves.append(
            remote(source, target.at[core], pre_sem.at[3 * i + 1], pre_sem.at[3 * i + 2], seat.partner)
        )
    for move in moves:
        move.start()
    for move in moves:
        move.wait()

    def fill(turn, chunk):
        slot = lax.rem(turn, SLOTS)
        shape = part.shape[1:]
        is_gain = (chunk == 0) & (core == 1)

        @pl.when(is_gain)
        def _():
            both = gain2[0] + gain2[1]
            padded = jnp.concatenate([both, jnp.zeros((120, both.shape[1]), jnp.float32)], axis=0)
            turned = jnp.transpose(padded)
            part[slot, :, :, :, :, pl.ds(0, 128)] = turned.reshape(shape[:-1] + (128,))
            part[slot, :, :, :, :, pl.ds(128, 256)] = jnp.zeros(shape[:-1] + (256,), jnp.float32)

        @pl.when(jnp.logical_not(is_gain))
        def _():
            which = left_of(chunk)
            columns = piece_columns(chunk, core)
            value = None
            for side in range(2):
                term = lax.dot_general(
                    left2[side, which],
                    right2[side, :, columns],
                    (((0,), (0,)), ((), ())),
                    preferred_element_type=jnp.float32,
                )
                value = term if value is None else value + term
            part[slot] = value.reshape(shape)

    work = Scatter(seat, chunks, fill, part, staged, landed, total, recv_sem, send_sem)
    lax.fori_loop(0, chunks + 3, lambda i, c: (work.round(i), c)[1], 0)


def gather_all(layers, packed):
    rows, width = packed.shape
    chunks = width // CHUNK
    held = pl.pallas_call(
        functools.partial(gather_kernel, layers, chunks),
        out_shape=jax.ShapeDtypeStruct((layers, 2, 2, 2 * rows, width), packed.dtype),
        in_specs=[pl.BlockSpec(memory_space=pltpu.VMEM)],
        out_specs=pl.BlockSpec(memory_space=pltpu.VMEM),
        scratch_shapes=[
            pltpu.VMEM((rows, width), packed.dtype),
            pltpu.SemaphoreType.DMA((2, chunks)),
            pltpu.SemaphoreType.DMA((chunks, 7)),
            pltpu.SemaphoreType.DMA((chunks, 11)),
        ],
        compiler_params=pltpu.CompilerParams(
            collective_id=0, has_side_effects=True, vmem_limit_bytes=60 * 1024 * 1024
        ),
    )(packed)
    return held.reshape(layers * 8 * rows, width)


def scatter_all(layers, lefts, rights, gains):
    kinds, tokens, depth = lefts.shape
    width = rights.shape[1]
    chunks = width // CHUNK
    rows = depth // (8 * layers)
    return pl.pallas_call(
        functools.partial(scatter_kernel, layers, chunks),
        out_shape=jax.ShapeDtypeStruct((rows, width), jnp.float32),
        in_specs=[pl.BlockSpec(memory_space=pl.ANY)] * 3,
        out_specs=pl.BlockSpec(memory_space=pltpu.VMEM),
        scratch_shapes=[
            pltpu.VMEM((2,) + lefts.shape, lefts.dtype),
            pltpu.VMEM((2,) + rights.shape, rights.dtype),
            pltpu.VMEM((2,) + gains.shape, gains.dtype),
            pltpu.VMEM((SLOTS, layers, 2, 2, 2 * rows, PIECE), jnp.float32),
            pltpu.VMEM((SLOTS, LANDING, 2 * rows, PIECE), jnp.bfloat16),
            pltpu.VMEM((chunks, LANDING, 2 * rows, PIECE), jnp.bfloat16),
            pltpu.SemaphoreType.DMA((9,)),
            pltpu.SemaphoreType.DMA((chunks, 8)),
            pltpu.SemaphoreType.DMA((SLOTS, 7)),
        ],
        compiler_params=pltpu.CompilerParams(
            collective_id=1, has_side_effects=True, vmem_limit_bytes=67043328
        ),
    )(lefts, rights, gains)
def per_device(
    block_input,
    segment_ids,
    output_grad,
    prenorm_one,
    inproj_one,
    outproj_one,
    midnorm_one,
    expand_one,
    shrink_one,
    prenorm_two,
    inproj_two,
    outproj_two,
    midnorm_two,
    expand_two,
    shrink_two,
):
    segment = segment_ids[0]
    positions = jnp.arange(segment.shape[0])
    allowed = (segment[:, None] == segment[None, :]) & (positions[None, :] <= positions[:, None])
    layer_one = (prenorm_one, inproj_one, outproj_one, midnorm_one, expand_one, shrink_one)
    layer_two = (prenorm_two, inproj_two, outproj_two, midnorm_two, expand_two, shrink_two)
    first_set = gather_weights(layer_one)
    inputs = block_input.astype(jnp.float32)
    first_parts = layer_forward(inputs, allowed, first_set, None)
    hidden = first_parts[12]
    first_values = first_parts[3]
    second_set = gather_weights(layer_two)
    second_parts = layer_forward(hidden, allowed, second_set, first_values)
    output = second_parts[12]
    second_back = gather_weights(layer_two)
    hidden_grad, kept_two, passed = layer_backward(
        hidden, allowed, second_back, first_values, output_grad.astype(jnp.float32), None
    )
    sums_two = sum_grads(kept_two)
    first_back = gather_weights(layer_one)
    input_grad, kept_one, unused_pass = layer_backward(
        inputs, allowed, first_back, None, hidden_grad, passed
    )
    sums_one = sum_grads(kept_one)
    return (
        output,
        input_grad,
        sums_one[0],
        sums_one[1],
        sums_one[2],
        sums_one[3],
        sums_one[4],
        sums_one[5],
        sums_two[0],
        sums_two[1],
        sums_two[2],
        sums_two[3],
        sums_two[4],
        sums_two[5],
    )


def per_device_linked(
    layers,
    block_input,
    segment_ids,
    output_grad,
    prenorm_one,
    inproj_one,
    outproj_one,
    midnorm_one,
    expand_one,
    shrink_one,
    prenorm_two,
    inproj_two,
    outproj_two,
    midnorm_two,
    expand_two,
    shrink_two,
):
    segment = segment_ids[0]
    positions = jnp.arange(segment.shape[0])
    allowed = (segment[:, None] == segment[None, :]) & (positions[None, :] <= positions[:, None])
    width = block_input.shape[1]
    rows = prenorm_one.shape[0]
    gains = jnp.stack([prenorm_one, midnorm_one, prenorm_two, midnorm_two], axis=1)
    packed = jnp.concatenate(
        [
            inproj_two[:, 2 * width :],
            gains,
            jnp.zeros((rows, PIECE - 4), jnp.bfloat16),
            inproj_one,
            outproj_one.T,
            expand_one,
            shrink_one.T,
            inproj_two[:, : 2 * width],
            outproj_two.T,
            expand_two,
            shrink_two.T,
        ],
        axis=1,
    )
    held = gather_all(layers, packed)
    hidden_width = expand_one.shape[1]

    def cut(start, size):
        return held[:, start : start + size]

    bases = [CHUNK + i * 0 for i in range(1)]
    base = CHUNK
    gain = held[:, PIECE : PIECE + 4]
    one = (
        gain[:, 0],
        cut(base, 3 * width),
        cut(base + 3 * width, width).T,
        gain[:, 1],
        cut(base + 4 * width, hidden_width),
        cut(base + 4 * width + hidden_width, hidden_width).T,
    )
    base = base + 4 * width + 2 * hidden_width
    two = (
        gain[:, 2],
        jnp.concatenate([cut(base, 2 * width), cut(0, width // 2)], axis=1),
        cut(base + 2 * width, width).T,
        gain[:, 3],
        cut(base + 3 * width, hidden_width),
        cut(base + 3 * width + hidden_width, hidden_width).T,
    )
    inputs = block_input.astype(jnp.float32)
    first_parts = layer_forward(inputs, allowed, one, None)
    hidden = first_parts[12]
    first_values = first_parts[3]
    second_parts = layer_forward(hidden, allowed, two, first_values)
    output = second_parts[12]
    hidden_grad, kept_two, passed = layer_backward(
        hidden, allowed, two, first_values, output_grad.astype(jnp.float32), None, second_parts
    )
    input_grad, kept_one, unused_pass = layer_backward(
        inputs, allowed, one, None, hidden_grad, passed, first_parts
    )

    def lefts(kept):
        return [kept[0], kept[2], kept[4], kept[6]]

    def rights(kept, proj):
        return [proj, kept[3], kept[5], kept[7]]

    rows_two = kept_two[1]
    left = jnp.stack(lefts(kept_one) + lefts(kept_two))
    right = jnp.concatenate(
        [rows_two[:, 2 * width :], jnp.zeros((rows_two.shape[0], PIECE), jnp.bfloat16)]
        + rights(kept_one, kept_one[1])
        + rights(kept_two, rows_two[:, : 2 * width]),
        axis=1,
    )
    gain_grads = jnp.stack([kept_one[8], kept_one[9], kept_two[8], kept_two[9]])
    gain_grads = jnp.concatenate([gain_grads, jnp.zeros_like(gain_grads)], axis=0)
    total = scatter_all(layers, left, right, gain_grads)

    def took(start, size):
        return total[:, start : start + size]

    def weights_of(base, proj):
        return (
            proj,
            took(base, width).T,
            took(base + width, hidden_width),
            took(base + width + hidden_width, hidden_width).T,
        )

    one_grads = weights_of(CHUNK + 3 * width, took(CHUNK, 3 * width))
    base = CHUNK + 4 * width + 2 * hidden_width
    two_grads = weights_of(
        base + 2 * width, jnp.concatenate([took(base, 2 * width), took(0, width // 2)], axis=1)
    )
    return (
        output,
        input_grad,
        took(PIECE, 1)[:, 0],
        one_grads[0],
        one_grads[1],
        took(PIECE + 1, 1)[:, 0],
        one_grads[2],
        one_grads[3],
        took(PIECE + 2, 1)[:, 0],
        two_grads[0],
        two_grads[1],
        took(PIECE + 3, 1)[:, 0],
        two_grads[2],
        two_grads[3],
    )


def solution(mesh):
    layers = mesh.shape["dp"]
    linked = layers == 4 and mesh.shape["fsdp"] == 8
    step = functools.partial(per_device_linked, layers) if linked else per_device
    return jax.shard_map(
        step,
        mesh=mesh,
        in_specs=(
            P(("dp", "fsdp"), None),
            P(("dp", "fsdp"), None),
            P(("dp", "fsdp"), None),
            P(("dp", "fsdp")),
            P(("dp", "fsdp"), None),
            P(None, ("dp", "fsdp")),
            P(("dp", "fsdp")),
            P(("dp", "fsdp"), None),
            P(None, ("dp", "fsdp")),
            P(("dp", "fsdp")),
            P(("dp", "fsdp"), None),
            P(None, ("dp", "fsdp")),
            P(("dp", "fsdp")),
            P(("dp", "fsdp"), None),
            P(None, ("dp", "fsdp")),
        ),
        out_specs=(
            P(("dp", "fsdp"), None),
            P(("dp", "fsdp"), None),
            P(("dp", "fsdp")),
            P(("dp", "fsdp"), None),
            P(None, ("dp", "fsdp")),
            P(("dp", "fsdp")),
            P(("dp", "fsdp"), None),
            P(None, ("dp", "fsdp")),
            P(("dp", "fsdp")),
            P(("dp", "fsdp"), None),
            P(None, ("dp", "fsdp")),
            P(("dp", "fsdp")),
            P(("dp", "fsdp"), None),
            P(None, ("dp", "fsdp")),
        ),
        check_vma=False,
    )
```

```python
import functools
import math
import types

import jax
import jax.numpy as jnp
from jax import lax
from jax.experimental import pallas as pl
from jax.experimental.pallas import tpu as pltpu
from jax.sharding import PartitionSpec as P

HEADS = 12


def layer_norm(inputs, gain):
    centred = inputs - jnp.mean(inputs, axis=-1, keepdims=True)
    spread = jnp.mean(centred * centred, axis=-1, keepdims=True)
    return centred * lax.rsqrt(spread + 1e-05) * gain


def gelu_tanh(value):
    return jax.nn.gelu(value, approximate=True)


def rows_product(left, right):
    return lax.dot_general(
        left, right, (((0,), (0,)), ((), ())), preferred_element_type=jnp.float32
    )


def cols_product(left, right):
    return lax.dot_general(
        left, right, (((1,), (1,)), ((), ())), preferred_element_type=jnp.float32
    )


def gather_weights(weights):
    prenorm, inproj, outproj, midnorm, expand, shrink = weights
    return (
        lax.all_gather(prenorm, ("dp", "fsdp"), axis=0, tiled=True),
        lax.all_gather(inproj, ("dp", "fsdp"), axis=0, tiled=True),
        lax.all_gather(outproj, ("dp", "fsdp"), axis=1, tiled=True),
        lax.all_gather(midnorm, ("dp", "fsdp"), axis=0, tiled=True),
        lax.all_gather(expand, ("dp", "fsdp"), axis=0, tiled=True),
        lax.all_gather(shrink, ("dp", "fsdp"), axis=1, tiled=True),
    )


def sum_grads(kept):
    (
        attn_in,
        proj_grad,
        branch_low,
        mixed,
        mlp_in,
        before_grad,
        out_low,
        active,
        prenorm_grad,
        midnorm_grad,
    ) = kept
    width = attn_in.shape[1]
    proj_width = proj_grad.shape[1]
    hidden_width = active.shape[1]

    def entries(value):
        return value[:, None]

    summed = lax.psum_scatter(
        jnp.concatenate(
            [
                rows_product(attn_in, proj_grad),
                rows_product(branch_low, mixed),
                rows_product(mlp_in, before_grad),
                rows_product(out_low, active),
                entries(prenorm_grad),
                entries(midnorm_grad),
            ],
            axis=1,
        ),
        ("dp", "fsdp"),
        scatter_dimension=0,
        tiled=True,
    )
    inproj_part = summed[:, :proj_width]
    outproj_part = summed[:, proj_width : proj_width + width].T
    expand_start = proj_width + width
    expand_part = summed[:, expand_start : expand_start + hidden_width]
    shrink_start = expand_start + hidden_width
    shrink_part = summed[:, shrink_start : shrink_start + hidden_width].T
    prenorm_part = summed[:, shrink_start + hidden_width]
    midnorm_part = summed[:, shrink_start + hidden_width + 1]
    return (prenorm_part, inproj_part, outproj_part, midnorm_part, expand_part, shrink_part)


def layer_forward(inputs, allowed, weights, first_values):
    prenorm, inproj, outproj, midnorm, expand, shrink = weights
    length, width = inputs.shape
    half = width // 2
    size = width // HEADS
    scale = 1.0 / math.sqrt(size)
    attn_in = layer_norm(inputs, prenorm.astype(jnp.float32)).astype(jnp.bfloat16)
    projected = jnp.dot(attn_in, inproj, preferred_element_type=jnp.float32)
    query = projected[:, :width].astype(jnp.bfloat16).reshape(length, HEADS, size)
    keys = projected[:, width : 2 * width].astype(jnp.bfloat16).reshape(length, HEADS, size)
    fresh = projected[:, 2 * width :].astype(jnp.bfloat16)
    if first_values is None:
        values = fresh
    else:
        values = jnp.concatenate([first_values[:, :half], fresh], axis=1)
    value_heads = values.reshape(length, HEADS, size)
    scores = jnp.einsum("qhd,khd->hqk", query, keys, preferred_element_type=jnp.float32) * scale
    scores = jnp.where(allowed[None], scores, -1000000000.0)
    highest = jnp.max(scores, axis=-1, keepdims=True)
    total = highest + jnp.log(jnp.sum(jnp.exp(scores - highest), axis=-1, keepdims=True))
    weights_full = jnp.exp(scores - total)
    probs = weights_full.astype(jnp.bfloat16)
    mixed = jnp.einsum("hqk,khd->qhd", probs, value_heads, preferred_element_type=jnp.float32)
    mixed = mixed.astype(jnp.bfloat16).reshape(length, width)
    middle = inputs + jnp.dot(mixed, outproj, preferred_element_type=jnp.float32)
    mlp_in = layer_norm(middle, midnorm.astype(jnp.float32)).astype(jnp.bfloat16)
    before = jnp.dot(mlp_in, expand, preferred_element_type=jnp.float32)
    active = gelu_tanh(before).astype(jnp.bfloat16)
    output = middle + jnp.dot(active, shrink, preferred_element_type=jnp.float32)
    return (
        attn_in,
        query,
        keys,
        fresh,
        value_heads,
        weights_full,
        probs,
        mixed,
        middle,
        mlp_in,
        before,
        active,
        output,
    )


def layer_backward(inputs, allowed, weights, first_values, incoming, carried):
    prenorm, inproj, outproj, midnorm, expand, shrink = weights
    length, width = inputs.shape
    half = width // 2
    size = width // HEADS
    scale = 1.0 / math.sqrt(size)
    parts = layer_forward(inputs, allowed, weights, first_values)
    (
        attn_in,
        query,
        keys,
        fresh,
        value_heads,
        weights_full,
        probs,
        mixed,
        middle,
        mlp_in,
        before,
        active,
        output,
    ) = parts
    out_low = incoming.astype(jnp.bfloat16)
    active_grad = cols_product(out_low, shrink)
    unused_gelu, gelu_pull = jax.vjp(gelu_tanh, before)
    before_grad = gelu_pull(active_grad)[0].astype(jnp.bfloat16)
    mlp_grad = cols_product(before_grad, expand)
    unused_mid, mid_pull = jax.vjp(layer_norm, middle, midnorm.astype(jnp.float32))
    middle_part, midnorm_grad = mid_pull(mlp_grad)
    middle_grad = incoming + middle_part
    branch_low = middle_grad.astype(jnp.bfloat16)
    mixed_grad = cols_product(branch_low, outproj).astype(jnp.bfloat16).reshape(length, HEADS, size)
    prob_grad = jnp.einsum(
        "qhd,khd->hqk", mixed_grad, value_heads, preferred_element_type=jnp.float32
    )
    value_grad = jnp.einsum(
        "hqk,qhd->khd", probs, mixed_grad, preferred_element_type=jnp.float32
    ).reshape(length, width)
    score_grad = weights_full * (
        prob_grad - jnp.sum(weights_full * prob_grad, axis=-1, keepdims=True)
    )
    score_low = score_grad.astype(jnp.bfloat16)
    query_grad = (
        (jnp.einsum("hqk,khd->qhd", score_low, keys, preferred_element_type=jnp.float32) * scale)
        .astype(jnp.bfloat16)
        .reshape(length, width)
    )
    keys_grad = (
        (jnp.einsum("hqk,qhd->khd", score_low, query, preferred_element_type=jnp.float32) * scale)
        .astype(jnp.bfloat16)
        .reshape(length, width)
    )
    if first_values is None:
        value_total = jnp.concatenate(
            [value_grad[:, :half] + carried, value_grad[:, half:]], axis=1
        )
        fresh_grad = value_total.astype(jnp.bfloat16)
        passed = None
    else:
        fresh_grad = value_grad[:, half:].astype(jnp.bfloat16)
        passed = value_grad[:, :half]
    proj_grad = jnp.concatenate([query_grad, keys_grad, fresh_grad], axis=1)
    attn_grad = cols_product(proj_grad, inproj)
    unused_in, in_pull = jax.vjp(layer_norm, inputs, prenorm.astype(jnp.float32))
    inputs_part, prenorm_grad = in_pull(attn_grad)
    kept = (
        attn_in,
        proj_grad,
        branch_low,
        mixed,
        mlp_in,
        before_grad,
        out_low,
        active,
        prenorm_grad,
        midnorm_grad,
    )
    return (middle_grad + inputs_part, kept, passed)


def per_device(
    block_input,
    segment_ids,
    output_grad,
    prenorm_one,
    inproj_one,
    outproj_one,
    midnorm_one,
    expand_one,
    shrink_one,
    prenorm_two,
    inproj_two,
    outproj_two,
    midnorm_two,
    expand_two,
    shrink_two,
):
    segment = segment_ids[0]
    positions = jnp.arange(segment.shape[0])
    allowed = (segment[:, None] == segment[None, :]) & (positions[None, :] <= positions[:, None])
    layer_one = (prenorm_one, inproj_one, outproj_one, midnorm_one, expand_one, shrink_one)
    layer_two = (prenorm_two, inproj_two, outproj_two, midnorm_two, expand_two, shrink_two)
    first_set = gather_weights(layer_one)
    inputs = block_input.astype(jnp.float32)
    first_parts = layer_forward(inputs, allowed, first_set, None)
    hidden = first_parts[12]
    first_values = first_parts[3]
    second_set = gather_weights(layer_two)
    second_parts = layer_forward(hidden, allowed, second_set, first_values)
    output = second_parts[12]
    second_back = gather_weights(layer_two)
    hidden_grad, kept_two, passed = layer_backward(
        hidden, allowed, second_back, first_values, output_grad.astype(jnp.float32), None
    )
    sums_two = sum_grads(kept_two)
    first_back = gather_weights(layer_one)
    input_grad, kept_one, unused_pass = layer_backward(
        inputs, allowed, first_back, None, hidden_grad, passed
    )
    sums_one = sum_grads(kept_one)
    return (
        output,
        input_grad,
        sums_one[0],
        sums_one[1],
        sums_one[2],
        sums_one[3],
        sums_one[4],
        sums_one[5],
        sums_two[0],
        sums_two[1],
        sums_two[2],
        sums_two[3],
        sums_two[4],
        sums_two[5],
    )


PIECE = 384
CHUNK = 2 * PIECE
CHUNKS = 24
REGIONS = 28
MESH = pl.DeviceIdType.MESH
FULL = slice(None)
GATHER_LAGS = (0, 2, 4, 6, 9, 12, 13)
SCATTER_LAGS = (0, 3, 5, 6, 7, 8, 10)
FIRST_TURN = 33
TICKS = FIRST_TURN + CHUNKS + SCATTER_LAGS[-1]


def when(condition, body):
    if isinstance(condition, bool):
        if condition:
            body()
    else:
        pl.when(condition)(body)


class Seat:
    def __init__(self, layers):
        self.layers = layers
        self.z = lax.axis_index("dp")
        place = lax.axis_index("fsdp")
        self.core = lax.rem(place, 2)
        self.x = lax.rem(lax.div(place, 2), 2)
        self.y = lax.div(place, 4)
        self.partner = (self.z, place + 1 - 2 * self.core)
        self.across_x = (self.z, place + 2 - 4 * self.x)
        self.across_y = (self.z, place + 4 - 8 * self.y)
        self.up = (self.z + 1, place)
        self.down = (self.z - 1, place)
        self.has_up = self.z < layers - 1
        self.has_down = self.z > 0

    def signal(self, semaphore, device):
        pl.semaphore_signal(semaphore, inc=1, device_id=device, device_id_type=MESH)

    def greet(self):
        barrier = pltpu.get_barrier_semaphore()
        for other in (self.partner, self.across_x, self.across_y):
            self.signal(barrier, other)
        when(self.has_up, lambda: self.signal(barrier, self.up))
        when(self.has_down, lambda: self.signal(barrier, self.down))
        inner = self.has_up & self.has_down
        when(inner, lambda: pl.semaphore_wait(barrier, 5))
        when(jnp.logical_not(inner), lambda: pl.semaphore_wait(barrier, 4))

    def give(self, credit, which):
        self.signal(credit.at[which, 0], self.across_x)
        self.signal(credit.at[which, 1], self.across_y)
        when(self.has_up, lambda: self.signal(credit.at[which, 2], self.up))
        when(self.has_down, lambda: self.signal(credit.at[which, 3], self.down))

    def take(self, credit, which):
        pl.semaphore_wait(credit.at[which, 0], 1)
        pl.semaphore_wait(credit.at[which, 1], 1)
        when(self.has_down, lambda: pl.semaphore_wait(credit.at[which, 2], 1))
        when(self.has_up, lambda: pl.semaphore_wait(credit.at[which, 3], 1))


def columns_of(start, size):
    return pl.ds(pl.multiple_of(start, 128), size)


def remote(source, target, send_sem, recv_sem, device):
    return pltpu.make_async_remote_copy(
        src_ref=source,
        dst_ref=target,
        send_sem=send_sem,
        recv_sem=recv_sem,
        device_id=device,
        device_id_type=MESH,
    )


def colour_of(chunk):
    step = lax.rem(chunk, 8)
    return jnp.where(
        (step == 2) | (step == 7), 2, jnp.where((step == 1) | (step == 4) | (step == 6), 1, 0)
    )


class Gather:
    def __init__(self, seat, m):
        self.seat, self.m = seat, m
        self.pre_sem, self.recv_sem, self.send_sem = m.pre_sem, m.gather_recv, m.gather_send

    def window(self, chunk, zs, ys, xs, core=None):
        core = self.seat.core if core is None else core
        return self.m.held.at[zs, ys, xs, :, columns_of(chunk * CHUNK + core * PIECE, PIECE)]

    def shard(self, ref, chunk, core):
        rows = pl.ds(pl.multiple_of(32 * lax.div(chunk, 4), 32), self.m.total.shape[0])
        return ref.at[rows, columns_of(CHUNK * lax.rem(chunk, 4) + PIECE * core, PIECE)]

    def swap(self, chunk, core):
        return remote(
            self.shard(self.m.own_rows, chunk, core),
            self.shard(self.m.other_rows, chunk, core),
            self.pre_sem.at[0, chunk],
            self.pre_sem.at[1, chunk],
            self.seat.partner,
        )

    def copy(self, chunk, zs, ys, xs, kind, arrival, device):
        window = self.window(chunk, zs, ys, xs)
        return remote(
            window, window, self.send_sem.at[chunk, kind], self.recv_sem.at[chunk, arrival], device
        )

    def up(self, chunk, origin, ys, xs):
        return self.copy(chunk, origin, ys, xs, origin, origin, self.seat.up)

    def down(self, chunk, origin, ys, xs):
        return self.copy(chunk, origin, ys, xs, 4 + origin, origin, self.seat.down)

    def merge(self, chunk):
        seat = self.seat
        self.swap(chunk, 1 - seat.core).wait_send()
        self.swap(chunk, seat.core).wait_recv()
        mine = self.shard(self.m.own_rows, chunk, seat.core)[...].astype(jnp.float32)
        theirs = self.shard(self.m.other_rows, chunk, seat.core)[...].astype(jnp.float32)
        first = seat.core == 0
        both = jnp.concatenate(
            [jnp.where(first, mine, theirs), jnp.where(first, theirs, mine)], axis=0
        )
        columns = columns_of(chunk * CHUNK + seat.core * PIECE, PIECE)
        self.m.held[seat.z, seat.y, seat.x, :, columns] = both.astype(jnp.bfloat16)

    def start_z(self, chunk, ys, xs):
        seat = self.seat
        when(seat.has_up, lambda: self.up(chunk, seat.z, ys, xs).start())
        when(seat.has_down, lambda: self.down(chunk, seat.z, ys, xs).start())

    def relay_z(self, chunk, step, ys, xs):
        seat = self.seat
        below, above = seat.z - 1 - step, seat.z + 1 + step

        def from_below():
            self.up(chunk, below, ys, xs).wait_recv()
            when(seat.has_up, lambda: self.up(chunk, below, ys, xs).start())

        def from_above():
            self.down(chunk, above, ys, xs).wait_recv()
            when(seat.has_down, lambda: self.down(chunk, above, ys, xs).start())

        when(below >= 0, from_below)
        when(above <= seat.layers - 1, from_above)

    def side(self, chunk, axis, zs, other):
        seat = self.seat
        if axis == "x":
            return self.copy(chunk, zs, other, seat.x, 8, 4, seat.across_x)
        return self.copy(chunk, zs, seat.y, other, 9, 5, seat.across_y)

    def side_arrives(self, chunk, axis, zs, other):
        seat = self.seat
        if axis == "x":
            self.copy(chunk, zs, other, 1 - seat.x, 8, 4, seat.across_x).wait_recv()
        else:
            self.copy(chunk, zs, 1 - seat.y, other, 9, 5, seat.across_y).wait_recv()

    def to_partner(self, chunk):
        return self.copy(chunk, FULL, FULL, FULL, 10, 6, self.seat.partner)

    def stage(self, chunk, number):
        seat = self.seat
        y, x = seat.y, seat.x

        def z_first(first, second, own_first):
            if number == 0:
                self.start_z(chunk, y, x)
            elif number <= 3:
                self.relay_z(chunk, number - 1, y, x)
            if number == 3:
                self.side(chunk, first, FULL, own_first).start()
            if number == 4:
                self.side_arrives(chunk, first, FULL, own_first)
                self.side(chunk, second, FULL, FULL).start()
            if number == 5:
                self.side_arrives(chunk, second, FULL, FULL)

        def z_last():
            if number == 0:
                self.side(chunk, "x", seat.z, y).start()
            if number == 1:
                self.side_arrives(chunk, "x", seat.z, y)
                self.side(chunk, "y", seat.z, FULL).start()
            if number == 2:
                self.side_arrives(chunk, "y", seat.z, FULL)
                self.start_z(chunk, FULL, FULL)
            if number >= 3:
                self.relay_z(chunk, number - 3, FULL, FULL)

        if number == 0:
            self.merge(chunk)
        if number <= 5:
            colour = colour_of(chunk)
            when(colour == 0, lambda: z_first("x", "y", y))
            when(colour == 1, lambda: z_first("y", "x", x))
            when(colour == 2, z_last)
        if number == 5:
            self.to_partner(chunk).start()
        if number == 6:
            window = self.window(chunk, FULL, FULL, FULL, 1 - seat.core)
            remote(
                window, window, self.send_sem.at[chunk, 10], self.recv_sem.at[chunk, 6], seat.partner
            ).wait_recv()

    def drain(self, chunk):
        seat = self.seat
        y, x = seat.y, seat.x

        def z_sends(ys, xs):
            for origin in range(seat.layers):
                when(
                    seat.has_up & (seat.z >= origin),
                    lambda: self.up(chunk, origin, ys, xs).wait_send(),
                )
                when(
                    seat.has_down & (seat.z <= origin),
                    lambda: self.down(chunk, origin, ys, xs).wait_send(),
                )

        def z_first(first, second, own_first):
            z_sends(y, x)
            self.side(chunk, first, FULL, own_first).wait_send()
            self.side(chunk, second, FULL, FULL).wait_send()

        def z_last():
            z_sends(FULL, FULL)
            self.side(chunk, "x", seat.z, y).wait_send()
            self.side(chunk, "y", seat.z, FULL).wait_send()

        colour = colour_of(chunk)
        when(colour == 0, lambda: z_first("x", "y", y))
        when(colour == 1, lambda: z_first("y", "x", x))
        when(colour == 2, z_last)
        self.to_partner(chunk).wait_send()

    def round(self, i):
        for number in reversed(range(7)):
            chunk = i - GATHER_LAGS[number]
            when((chunk >= 0) & (chunk < CHUNKS), functools.partial(self.stage, chunk, number))


def chunk_at(turn):
    chunk = turn - 23
    for end, shift in ((23, -19), (20, -15), (19, -10), (15, -2), (11, 4), (9, 7), (8, 12), (4, 20)):
        chunk = jnp.where(turn < end, turn + shift, chunk)
    return chunk


def region_at(turn):
    region = turn - 19
    for end, shift in ((23, -14), (19, -6), (15, 0), (13, 3), (12, 8), (8, 16), (4, 24)):
        region = jnp.where(turn < end, turn + shift, region)
    return jnp.where(turn == 13, 13, region)


class Scatter:
    def __init__(self, seat, m, fill):
        self.seat, self.m, self.fill = seat, m, fill
        self.recv_sem, self.send_sem = m.scatter_recv, m.scatter_send

    def part(self, turn):
        return columns_of(region_at(turn) * CHUNK + PIECE, PIECE)

    def landing(self, turn):
        return columns_of(region_at(turn) * CHUNK, PIECE)

    def rare(self, turn):
        return 2 * lax.div(turn, 8) + lax.div(lax.rem(turn, 8), 7)

    def sent(self, turn, zs, ys, xs, target, kind, arrival, device):
        return remote(
            self.m.held.at[zs, ys, xs, :, self.part(turn)],
            target,
            self.send_sem.at[turn, kind],
            self.recv_sem.at[turn, arrival],
            device,
        )

    def add(self, turn, zs, ys, xs, landed):
        columns = self.part(turn)
        value = self.m.held[zs, ys, xs, :, columns].astype(jnp.float32)
        value = value + landed[...].astype(jnp.float32)
        self.m.held[zs, ys, xs, :, columns] = value.astype(jnp.bfloat16)

    def side(self, turn, axis, zs, other, target):
        seat = self.seat
        if axis == "x":
            return self.sent(turn, zs, other, 1 - seat.x, target, 0, 0, seat.across_x)
        return self.sent(turn, zs, 1 - seat.y, other, target, 1, 1, seat.across_y)

    def finish_side(self, turn, axis, zs, other, target):
        seat = self.seat
        self.side(turn, axis, zs, other, target).wait_recv()
        if axis == "x":
            self.add(turn, zs, other, seat.x, target)
        else:
            self.add(turn, zs, seat.y, other, target)

    def first_spot(self, turn):
        return self.m.held.at[:, 0, :, :, self.landing(turn)]

    def second_spot(self, turn):
        return self.m.held.at[:, 1, 0, :, self.landing(turn)]

    def late_z_spot(self, turn, goal):
        return self.m.held.at[goal, 1, 1, :, self.landing(turn)]

    def late_own_spot(self, turn):
        return self.m.extra.at[turn]

    def early_z_spot(self, turn, goal):
        return self.m.held.at[goal, :, :, :, self.landing(turn)]

    def early_own_spot(self, turn):
        return self.m.extra_four.at[self.rare(turn)]

    def early_y_spot(self, turn):
        return self.m.extra_two.at[self.rare(turn)]

    def early_x_spot(self, turn):
        return self.m.extra.at[turn]

    def step_z(self, turn, step, spot, own_spot, ys, xs):
        seat = self.seat
        layers = seat.layers

        def send_up(goal):
            return self.sent(turn, goal, ys, xs, spot(turn, goal), 2 + goal, 2 + goal, seat.up)

        def send_down(goal):
            return self.sent(turn, goal, ys, xs, spot(turn, goal), 2 + goal, 2 + goal, seat.down)

        def send_down_own(goal):
            return self.sent(
                turn, goal, ys, xs, own_spot(turn), 2 + goal, 2 + layers, seat.down
            )

        def arrived(goal, window, arrival):
            remote(
                window,
                window,
                self.send_sem.at[turn, 0],
                self.recv_sem.at[turn, 2 + arrival],
                seat.partner,
            ).wait_recv()
            self.add(turn, goal, ys, xs, window)

        def upward():
            for goal in range(1, layers):

                def one(goal=goal):
                    when(seat.has_down, lambda: arrived(goal, spot(turn, goal), goal))
                    when(seat.z < goal, lambda: send_up(goal).start())

                when(seat.z <= goal, one)

        def downward():
            for goal in range(layers - 1):

                def one(goal=goal):
                    when(
                        seat.has_up & (seat.z != goal),
                        lambda: arrived(goal, spot(turn, goal), goal),
                    )
                    when(
                        seat.has_up & (seat.z == goal),
                        lambda: arrived(goal, own_spot(turn), layers),
                    )
                    when(seat.z > goal + 1, lambda: send_down(goal).start())
                    when(seat.z == goal + 1, lambda: send_down_own(goal).start())

                when(seat.z >= goal, one)

        when(seat.z == step, upward)
        when(seat.z == layers - 1 - step, downward)

    def finished(self, turn):
        return self.m.finished.at[lax.rem(turn, 4)]

    def hand_over(self, turn):
        rows = self.m.total.shape[0]
        theirs = pl.ds(pl.multiple_of((1 - self.seat.core) * rows, 8), rows)
        columns = columns_of(chunk_at(turn) * CHUNK + self.seat.core * PIECE, PIECE)
        return remote(
            self.finished(turn).at[theirs],
            self.m.total.at[:, columns],
            self.send_sem.at[turn, 6],
            self.recv_sem.at[turn, 7],
            self.seat.partner,
        )

    def stage(self, turn, number):
        seat = self.seat
        y, x, z = seat.y, seat.x, seat.z

        def z_last(first, second, own_second):
            if number == 0:
                self.side(turn, first, FULL, FULL, self.first_spot(turn)).start()
            if number == 1:
                self.finish_side(turn, first, FULL, FULL, self.first_spot(turn))
                self.side(turn, second, FULL, own_second, self.second_spot(turn)).start()
            if number == 2:
                self.finish_side(turn, second, FULL, own_second, self.second_spot(turn))
            if number >= 2:
                self.step_z(turn, number - 2, self.late_z_spot, self.late_own_spot, y, x)

        def z_first():
            if number <= 3:
                self.step_z(turn, number, self.early_z_spot, self.early_own_spot, FULL, FULL)
            if number == 3:
                self.side(turn, "y", z, FULL, self.early_y_spot(turn)).start()
            if number == 4:
                self.finish_side(turn, "y", z, FULL, self.early_y_spot(turn))
                self.side(turn, "x", z, y, self.early_x_spot(turn)).start()
            if number == 5:
                self.finish_side(turn, "x", z, y, self.early_x_spot(turn))

        if number == 0:
            self.fill(turn, chunk_at(turn), self.part(turn))
        if number <= 5:
            colour = colour_of(turn)
            when(colour == 0, lambda: z_last("y", "x", y))
            when(colour == 1, lambda: z_last("x", "y", x))
            when(colour == 2, z_first)
        if number == 5:
            rows = self.m.total.shape[0]
            ready = self.finished(turn)
            ready[...] = self.m.held[z, y, x, :, self.part(turn)].astype(jnp.float32)
            mine = pl.ds(pl.multiple_of(seat.core * rows, 8), rows)
            columns = columns_of(chunk_at(turn) * CHUNK + seat.core * PIECE, PIECE)
            self.m.total[:, columns] = ready[mine, :]
            self.hand_over(turn).start()
        if number == 6:
            self.hand_over(turn).wait_send()
            columns = columns_of(chunk_at(turn) * CHUNK + (1 - seat.core) * PIECE, PIECE)
            window = self.m.total.at[:, columns]
            remote(
                window, window, self.send_sem.at[turn, 6], self.recv_sem.at[turn, 7], seat.partner
            ).wait_recv()
            self.drain(turn)

    def drain(self, turn):
        seat = self.seat
        y, x, z = seat.y, seat.x, seat.z

        def z_sends(spot, ys, xs):
            for goal in range(seat.layers):

                def one(goal=goal):
                    self.sent(
                        turn, goal, ys, xs, spot(turn, goal), 2 + goal, 2 + goal, seat.partner
                    ).wait_send()

                when(seat.z != goal, one)

        def z_last(first, second, own_second):
            self.side(turn, first, FULL, FULL, self.first_spot(turn)).wait_send()
            self.side(turn, second, FULL, own_second, self.second_spot(turn)).wait_send()
            z_sends(self.late_z_spot, y, x)

        def z_first():
            z_sends(self.early_z_spot, FULL, FULL)
            self.side(turn, "y", z, FULL, self.early_y_spot(turn)).wait_send()
            self.side(turn, "x", z, y, self.early_x_spot(turn)).wait_send()

        colour = colour_of(turn)
        when(colour == 0, lambda: z_last("y", "x", y))
        when(colour == 1, lambda: z_last("x", "y", x))
        when(colour == 2, z_first)

    def round(self, i):
        for number in reversed(range(7)):
            turn = i - SCATTER_LAGS[number]
            when((turn >= 0) & (turn < CHUNKS), functools.partial(self.stage, turn, number))


def nn_product(left, right):
    return lax.dot_general(
        left, right, (((1,), (0,)), ((), ())), preferred_element_type=jnp.float32
    )


def nt_product(left, right):
    return lax.dot_general(
        left, right, (((1,), (1,)), ((), ())), preferred_element_type=jnp.float32
    )


def tn_product(left, right):
    return lax.dot_general(
        left, right, (((0,), (0,)), ((), ())), preferred_element_type=jnp.float32
    )


def normal(value):
    centred = value - jnp.mean(value, axis=-1, keepdims=True)
    spread = jnp.mean(centred * centred, axis=-1, keepdims=True)
    rate = lax.rsqrt(spread + 1e-05)
    return centred * rate, rate


def loop(count, body):
    lax.fori_loop(0, count, lambda i, c: (body(i), c)[1], 0)


class Layers:
    def __init__(self, seat, m):
        self.seat, self.m = seat, m
        self.width = m.block.shape[1]
        self.scale = 1.0 / math.sqrt(self.width // HEADS)

    def weight(self, chunk):
        return self.m.held[:, :, :, :, columns_of(chunk * CHUNK, CHUNK)].reshape(
            self.width, CHUNK
        )

    def gain(self, row):
        return self.m.gains[pl.ds(row, 1), :]

    def begin(self):
        m = self.m
        columns = m.held[:, :, :, :, pl.ds(PIECE, 128)].reshape(self.width, 128)
        turned = jnp.transpose(columns.astype(jnp.float32))
        m.gains[...] = turned[:8]
        m.gain_grads[...] = jnp.zeros_like(m.gain_grads)
        segment = m.segment[...].astype(jnp.float32)
        tokens = segment.shape[1]
        across = jnp.broadcast_to(segment, (tokens, tokens))
        along = jnp.transpose(across)
        later = lax.broadcasted_iota(jnp.int32, (tokens, tokens), 1)
        now = lax.broadcasted_iota(jnp.int32, (tokens, tokens), 0)
        allowed = (along == across) & (later <= now)
        m.allowed[...] = jnp.where(allowed, 1.0, 0.0)
        m.block_load.wait()
        value = m.mixed_grad[...].astype(jnp.float32)
        m.entered[0] = value
        m.attn_in[0] = (normal(value)[0] * self.gain(0)).astype(jnp.bfloat16)

    def project(self, layer, part, chunk):
        m = self.m
        value = nn_product(m.attn_in[layer], self.weight(chunk))
        m.proj[layer, :, columns_of(part * CHUNK, CHUNK)] = value.astype(jnp.bfloat16)

    def project_fresh(self):
        m = self.m
        half = self.width // 2
        weight = m.held[:, :, :, :, pl.ds(0, PIECE)].reshape(self.width, PIECE)
        value = nn_product(m.attn_in[1], weight)
        m.proj[1, :, pl.ds(2 * self.width + half, half)] = value.astype(jnp.bfloat16)
        m.proj[1, :, pl.ds(2 * self.width, half)] = m.proj[0, :, pl.ds(2 * self.width, half)]

    def heads(self, layer, pair):
        m = self.m
        parts = []
        for i in range(3):
            parts.append(m.proj[layer, :, columns_of(i * self.width + pair * 128, 128)])
        return parts

    def own_lanes(self, which):
        lane = lax.broadcasted_iota(jnp.int32, (self.m.block.shape[0], 128), 1)
        return (lane < 64) if which == 0 else (lane >= 64)

    def only(self, which, value):
        return jnp.where(self.own_lanes(which), value, jnp.zeros_like(value))

    def probabilities(self, query, keys):
        scores = nt_product(query, keys) * self.scale
        scores = jnp.where(self.m.allowed[...] > 0.5, scores, -1000000000.0)
        highest = jnp.max(scores, axis=-1, keepdims=True)
        powers = jnp.exp(scores - highest)
        return powers * (1.0 / jnp.sum(powers, axis=-1, keepdims=True))

    def attend(self, layer):
        m = self.m

        def pair(p):
            query, keys, values = self.heads(layer, p)
            mixed = []
            for which in range(2):
                probs = self.probabilities(self.only(which, query), keys)
                mixed.append(nn_product(probs.astype(jnp.bfloat16), values))
            m.mixed[layer, :, columns_of(p * 128, 128)] = jnp.where(
                self.own_lanes(0), mixed[0], mixed[1]
            ).astype(jnp.bfloat16)

        loop(HEADS // 2, pair)

    def project_out(self, layer, chunk):
        m = self.m
        middle = m.entered[layer] + nt_product(m.mixed[layer], self.weight(chunk))
        m.middle[layer] = middle
        m.mlp_in[layer] = (normal(middle)[0] * self.gain(2 * layer + 1)).astype(jnp.bfloat16)

    def expand(self, layer, part, chunk):
        m = self.m
        value = nn_product(m.mlp_in[layer], self.weight(chunk))
        root = math.sqrt(2.0 / math.pi)
        square = value * value
        bend = jnp.tanh(root * value * (1.0 + 0.044715 * square))
        columns = columns_of(part * CHUNK, CHUNK)
        m.active[layer, :, columns] = (0.5 * value * (1.0 + bend)).astype(jnp.bfloat16)
        slope = 0.5 * (1.0 + bend) + 0.5 * value * (1.0 - bend * bend) * (
            root * (1.0 + 3.0 * 0.044715 * square)
        )
        m.slope[layer, :, columns] = slope.astype(jnp.bfloat16)

    def shrink(self, layer, part, chunk):
        m = self.m
        term = nt_product(m.active[layer, :, columns_of(part * CHUNK, CHUNK)], self.weight(chunk))

        @pl.when(part == 0)
        def _():
            m.output[...] = m.middle[layer] + term

        @pl.when(part > 0)
        def _():
            m.output[...] += term

        @pl.when((part == 3) & (layer == 0))
        def _():
            value = m.output[...]
            m.entered[1] = value
            m.attn_in[1] = (normal(value)[0] * self.gain(2)).astype(jnp.bfloat16)

    def forward(self, chunk):
        second = chunk >= 13
        layer = jnp.where(second, 1, 0)
        begins = [jnp.where(second, b, a) for a, b in ((1, 13), (4, 15), (5, 16), (9, 20))]
        when(chunk == 0, self.begin)
        when(
            (chunk >= begins[0]) & (chunk < begins[1]),
            lambda: self.project(layer, chunk - begins[0], chunk),
        )
        when(chunk == 14, self.project_fresh)
        when(chunk == begins[1] - 1, lambda: self.attend(layer))
        when(chunk == begins[1], lambda: self.project_out(layer, chunk))
        when(
            (chunk >= begins[2]) & (chunk < begins[3]),
            lambda: self.expand(layer, chunk - begins[2], chunk),
        )
        when(
            (chunk >= begins[3]) & (chunk < begins[3] + 4),
            lambda: self.shrink(layer, chunk - begins[3], chunk),
        )


    def exchange(self, layer, item):
        m = self.m
        width = self.width
        pairs = (
            (m.out_low.at[layer], m.other_out_low),
            (m.active.at[layer], m.other_active),
            (m.mlp_in.at[layer], m.other_mlp_in),
            (m.slope.at[layer], m.other_slope),
            (m.mixed.at[layer], m.other_mixed),
            (m.branch.at[layer], m.other_branch),
            (m.attn_in.at[layer], m.other_attn_in.at[layer]),
            (m.proj.at[layer, :, pl.ds(0, 2 * width)], m.other_proj.at[:, pl.ds(0, 2 * width)]),
            (m.proj.at[0, :, pl.ds(2 * width, width)], m.other_proj.at[:, pl.ds(2 * width, width)]),
            (m.proj.at[1, :, pl.ds(2 * width + width // 2, width // 2)], m.other_fresh),
            (m.gain_grads, m.other_gain_grads),
        )
        source, target = pairs[item]
        return remote(
            source,
            target,
            m.pair_sem.at[0, layer, item],
            m.pair_sem.at[1, layer, item],
            self.seat.partner,
        )

    def hidden_back(self, layer):
        m = self.m

        def part(j):
            columns = columns_of(j * CHUNK, CHUNK)
            grad = nn_product(
                m.out_low[layer], self.weight(jnp.where(layer == 1, 20, 9) + j)
            )
            slope = m.slope[layer, :, columns].astype(jnp.float32)
            m.slope[layer, :, columns] = (grad * slope).astype(jnp.bfloat16)

        loop(4, part)

    def norm_back(self, value, grad, row):
        m = self.m
        unit, rate = normal(value)
        m.gain_grads[pl.ds(row, 1), :] = jnp.sum(grad * unit, axis=0, keepdims=True)
        scaled = grad * self.gain(row)
        return rate * (
            scaled
            - jnp.mean(scaled, axis=-1, keepdims=True)
            - unit * jnp.mean(scaled * unit, axis=-1, keepdims=True)
        )

    def middle_back(self, layer):
        m = self.m
        first = jnp.where(layer == 1, 16, 5)
        grad = None
        for j in range(4):
            term = nt_product(m.slope[layer, :, pl.ds(j * CHUNK, CHUNK)], self.weight(first + j))
            grad = term if grad is None else grad + term
        m.grad[...] += self.norm_back(m.middle[layer], grad, 2 * layer + 1)
        low = m.grad[...].astype(jnp.bfloat16)
        m.branch[layer] = low
        chunk = jnp.where(layer == 1, 15, 4)
        m.mixed_grad[...] = nn_product(low, self.weight(chunk)).astype(jnp.bfloat16)

    def attend_back(self, layer):
        m = self.m
        width = self.width

        def pair(p):
            query, keys, values = self.heads(layer, p)
            above = m.mixed_grad[:, columns_of(p * 128, 128)]
            grads = []
            for which in range(2):
                probs32 = self.probabilities(self.only(which, query), keys)
                probs = probs32.astype(jnp.bfloat16)
                prob_grad = nt_product(self.only(which, above), values)
                value_grad = tn_product(probs, above)
                score_grad = probs32 * (
                    prob_grad - jnp.sum(probs32 * prob_grad, axis=-1, keepdims=True)
                )
                low = score_grad.astype(jnp.bfloat16)
                grads.append(
                    (
                        nn_product(low, keys) * self.scale,
                        tn_product(low, query) * self.scale,
                        value_grad,
                    )
                )
            query_grad, keys_grad, value_grad = [
                jnp.where(self.own_lanes(0), one, two) for one, two in zip(*grads)
            ]
            m.proj[layer, :, columns_of(p * 128, 128)] = query_grad.astype(jnp.bfloat16)
            m.proj[layer, :, columns_of(width + p * 128, 128)] = keys_grad.astype(jnp.bfloat16)
            columns = columns_of(2 * width + p * 128, 128)
            early = p < HEADS // 4
            carried = columns_of(lax.rem(p, HEADS // 4) * 128, 128)

            @pl.when(early & (layer == 1))
            def _():
                m.carried[:, carried] = value_grad

            @pl.when(early & (layer == 0))
            def _():
                m.proj[layer, :, columns] = (value_grad + m.carried[:, carried]).astype(
                    jnp.bfloat16
                )

            @pl.when(jnp.logical_not(early))
            def _():
                m.proj[layer, :, columns] = value_grad.astype(jnp.bfloat16)

        loop(HEADS // 2, pair)

    def enter_back(self, layer):
        m = self.m
        width, half = self.width, self.width // 2
        first = jnp.where(layer == 1, 13, 1)
        grad = nt_product(m.proj[layer, :, pl.ds(0, width)], self.weight(first))
        grad += nt_product(m.proj[layer, :, pl.ds(width, width)], self.weight(first + 1))
        m.scratch[...] = grad

        @pl.when(layer == 1)
        def _():
            weight = m.held[:, :, :, :, pl.ds(0, PIECE)].reshape(width, PIECE)
            m.scratch[...] += nt_product(m.proj[1, :, pl.ds(2 * width + half, half)], weight)

        @pl.when(layer == 0)
        def _():
            m.scratch[...] += nt_product(m.proj[0, :, pl.ds(2 * width, width)], self.weight(3))

        m.grad[...] += self.norm_back(m.entered[layer], m.scratch[...], 2 * layer)

        @pl.when(layer == 1)
        def _():
            m.out_low[0] = m.grad[...].astype(jnp.bfloat16)

    def fill(self, turn, chunk, target):
        m = self.m
        seat = self.seat
        second = chunk >= 13
        layer = jnp.where(second, 1, 0)
        begins = [jnp.where(second, b, a) for a, b in ((1, 13), (4, 15), (5, 16), (9, 20))]
        shape = m.held.shape[:4]

        def store(value):
            m.held[:, :, :, :, target] = value.astype(jnp.bfloat16).reshape(shape + (PIECE,))

        def product(begin, left, other_left, right, other_right):
            def run():
                columns = columns_of((chunk - begin) * CHUNK + seat.core * PIECE, PIECE)
                store(
                    tn_product(left[...], right[:, columns])
                    + tn_product(other_left[...], other_right[:, columns])
                )

            return run

        def arrive(items):
            for item in items:
                copy = self.exchange(layer, item)
                copy.wait_send()
                copy.wait_recv()

        def arrive_fixed(where, item):
            copy = self.exchange(where, item)
            copy.wait_send()
            copy.wait_recv()

        at_proj = (chunk >= begins[0]) & (chunk < begins[1])
        at_out = chunk == begins[1]
        at_expand = (chunk >= begins[2]) & (chunk < begins[3])
        at_shrink = chunk >= begins[3]
        at_shrink = at_shrink & (chunk < begins[3] + 4)
        when(at_shrink & (chunk == begins[3]), lambda: arrive((0, 1)))
        when(at_expand & (chunk == begins[2]), lambda: arrive((2, 3)))
        when(at_out, lambda: arrive((4, 5)))

        @pl.when(at_proj & (chunk == begins[0]))
        def _():
            arrive((6, 7))
            when(layer == 1, lambda: arrive_fixed(1, 9))
            when(layer == 0, lambda: arrive_fixed(0, 8))

        when(
            at_shrink,
            product(
                begins[3], m.out_low.at[layer], m.other_out_low, m.active.at[layer], m.other_active
            ),
        )
        when(
            at_expand,
            product(
                begins[2], m.mlp_in.at[layer], m.other_mlp_in, m.slope.at[layer], m.other_slope
            ),
        )
        when(
            at_out,
            product(
                begins[1], m.branch.at[layer], m.other_branch, m.mixed.at[layer], m.other_mixed
            ),
        )
        when(
            at_proj,
            product(
                begins[0],
                m.attn_in.at[layer],
                m.other_attn_in.at[layer],
                m.proj.at[layer],
                m.other_proj,
            ),
        )

        @pl.when((chunk == 0) & (seat.core == 0))
        def _():
            own = m.proj[1, :, pl.ds(2 * self.width + PIECE, PIECE)]
            store(
                tn_product(m.attn_in[1], own) + tn_product(m.other_attn_in[1], m.other_fresh[...])
            )

        @pl.when(chunk == 0)
        def _():
            arrive_fixed(0, 10)

        @pl.when((chunk == 0) & (seat.core == 1))
        def _():
            both = m.gain_grads[...] + m.other_gain_grads[...]
            padded = jnp.concatenate(
                [both, jnp.zeros((120, both.shape[1]), jnp.float32)], axis=0
            )
            turned = jnp.transpose(padded)
            wide = jnp.concatenate(
                [turned, jnp.zeros((turned.shape[0], PIECE - 128), jnp.float32)], axis=1
            )
            store(wide)

    def backward(self, tick):
        m = self.m
        seat = self.seat

        def send(layer, *items):
            for item in items:
                self.exchange(layer, item).start()

        @pl.when(tick == 20)
        def _():
            m.above_load.wait()
            m.grad[...] = m.out_low[1].astype(jnp.float32)

        when(tick == FIRST_TURN - 1, lambda: send(1, 0, 1, 2, 4, 6))

        @pl.when(tick == 44)
        def _():
            pl.semaphore_wait(m.pair_credit.at[0], 1)
            send(0, 0, 1, 2, 4, 6)

        @pl.when((tick == 36) | (tick == 44))
        def _():
            layer = jnp.where(tick == 36, 1, 0)
            self.hidden_back(layer)
            send(layer, 3)
            when(tick == 36, lambda: seat.give(m.credit, 0))
            when(tick == 44, lambda: seat.give(m.credit, 3))

        @pl.when((tick == 37) | (tick == 46))
        def _():
            layer = jnp.where(tick == 37, 1, 0)
            self.middle_back(layer)
            send(layer, 5)
            when(tick == 37, lambda: seat.give(m.credit, 1))
            when(tick == 46, lambda: seat.give(m.credit, 4))

        @pl.when((tick == 38) | (tick == 48))
        def _():
            layer = jnp.where(tick == 38, 1, 0)
            self.attend_back(layer)
            send(layer, 7)
            when(tick == 38, lambda: send(1, 9))
            when(tick == 48, lambda: send(0, 8))

        @pl.when((tick == 39) | (tick == 50))
        def _():
            layer = jnp.where(tick == 39, 1, 0)
            self.enter_back(layer)
            when(tick == 39, lambda: seat.give(m.credit, 2))
            when(tick == 50, lambda: send(0, 10))


def whole_kernel(layers, names, *refs):
    m = types.SimpleNamespace(**dict(zip(names, refs)))
    seat = Seat(layers)
    seat.greet()
    m.own_rows, m.other_rows = m.other_slope, m.other_active
    gather = Gather(seat, m)
    model = Layers(seat, m)
    scatter = Scatter(seat, m, model.fill)

    rows = m.total.shape[0]
    pieces = [(m.inproj_two, 2 * m.block.shape[1], PIECE, 0, 0), (m.gain_rows, 0, PIECE, 0, 1)]
    chunk = 1
    for source, wide in (
        (m.inproj_one, 3),
        (m.outproj_one, 1),
        (m.expand_one, 4),
        (m.shrink_one, 4),
        (m.inproj_two, 2),
        (m.outproj_two, 1),
        (m.expand_two, 4),
        (m.shrink_two, 4),
    ):
        for j in range(wide):
            pieces.append((source, j * CHUNK, CHUNK, chunk, 0))
            chunk += 1
    loads = []
    for i, (source, start, size, chunk, side) in enumerate(pieces):
        place = (slice(32 * (chunk // 4), 32 * (chunk // 4) + rows),)
        place += (pl.ds(CHUNK * (chunk % 4) + PIECE * side, size),)
        loads.append(
            pltpu.make_async_copy(
                source.at[:, pl.ds(start, size)], m.own_rows.at[place], m.load_sem.at[i]
            )
        )
    m.block_load = pltpu.make_async_copy(m.block, m.mixed_grad, m.load_sem.at[CHUNKS + 1])
    m.above_load = pltpu.make_async_copy(m.above, m.out_low.at[1], m.load_sem.at[CHUNKS + 2])
    for load in loads + [m.block_load, m.above_load]:
        load.start()
    for i, load in enumerate(loads):
        load.wait()
        if i >= 1:
            gather.swap(pieces[i][3], 1 - seat.core).start()

    def tick(t):
        when(t < CHUNKS + GATHER_LAGS[-1], lambda: gather.round(t))
        chunk = t - GATHER_LAGS[-1]
        when((chunk >= 0) & (chunk < CHUNKS), lambda: model.forward(chunk))
        when(t == CHUNKS + GATHER_LAGS[-1] - 1, lambda: loop(CHUNKS, gather.drain))
        model.backward(t)
        turn = t - FIRST_TURN
        for which, first in enumerate((4, 8, 12, 15, 19)):
            when(turn == first, lambda which=which: seat.take(m.credit, which))
        scatter.round(turn)
        when(turn == 10, lambda: seat.signal(m.pair_credit.at[0], seat.partner))

    loop(TICKS, tick)


def run_layers(layers, block, segment, above, gain_rows, weights):
    tokens, width = block.shape
    rows, hidden = weights[2].shape[0], weights[2].shape[1]
    low, wide = jnp.bfloat16, jnp.float32
    names, args, in_specs = [], [], []
    for name, value in (("block", block), ("segment", segment), ("above", above)):
        names.append(name)
        args.append(value)
        space = pltpu.VMEM if name == "segment" else pl.ANY
        in_specs.append(pl.BlockSpec(memory_space=space))
    matrices = ("inproj", "outproj", "expand", "shrink")
    for name, value in zip(
        ["gain_rows"] + [n + end for end in ("_one", "_two") for n in matrices],
        [gain_rows] + list(weights),
    ):
        names.append(name)
        args.append(value)
        in_specs.append(pl.BlockSpec(memory_space=pl.ANY))
    outs = (
        ("output", (tokens, width), wide),
        ("grad", (tokens, width), wide),
        ("total", (rows, CHUNKS * CHUNK), wide),
    )
    both = 2 * rows
    scratch = (
        ("held", (layers, 2, 2, both, REGIONS * CHUNK), low),
        ("extra", (CHUNKS, both, PIECE), low),
        ("extra_four", (CHUNKS // 4, 2, 2, both, PIECE), low),
        ("extra_two", (CHUNKS // 4, 2, both, PIECE), low),
        ("finished", (4, both, PIECE), wide),
        ("gains", (8, width), wide),
        ("gain_grads", (8, width), wide),
        ("other_gain_grads", (8, width), wide),
        ("allowed", (tokens, tokens), wide),
        ("entered", (2, tokens, width), wide),
        ("attn_in", (2, tokens, width), low),
        ("proj", (2, tokens, 3 * width), low),
        ("mixed", (2, tokens, width), low),
        ("middle", (2, tokens, width), wide),
        ("mlp_in", (2, tokens, width), low),
        ("active", (2, tokens, hidden), low),
        ("slope", (2, tokens, hidden), low),
        ("out_low", (2, tokens, width), low),
        ("branch", (2, tokens, width), low),
        ("mixed_grad", (tokens, width), low),
        ("carried", (tokens, width // 2), wide),
        ("scratch", (tokens, width), wide),
        ("other_out_low", (tokens, width), low),
        ("other_active", (tokens, hidden), low),
        ("other_mlp_in", (tokens, width), low),
        ("other_slope", (tokens, hidden), low),
        ("other_mixed", (tokens, width), low),
        ("other_branch", (tokens, width), low),
        ("other_attn_in", (2, tokens, width), low),
        ("other_proj", (tokens, 3 * width), low),
        ("other_fresh", (tokens, width // 2), low),
    )
    waits = (
        ("load_sem", pltpu.SemaphoreType.DMA((CHUNKS + 3,))),
        ("pre_sem", pltpu.SemaphoreType.DMA((2, CHUNKS))),
        ("gather_recv", pltpu.SemaphoreType.DMA((CHUNKS, 7))),
        ("gather_send", pltpu.SemaphoreType.DMA((CHUNKS, 11))),
        ("scatter_recv", pltpu.SemaphoreType.DMA((CHUNKS, 8))),
        ("scatter_send", pltpu.SemaphoreType.DMA((CHUNKS, 7))),
        ("pair_sem", pltpu.SemaphoreType.DMA((2, 2, 11))),
        ("credit", pltpu.SemaphoreType.REGULAR((5, 4))),
        ("pair_credit", pltpu.SemaphoreType.REGULAR((1,))),
    )
    names += [n for n, _, _ in outs] + [n for n, _, _ in scratch] + [n for n, _ in waits]
    return pl.pallas_call(
        functools.partial(whole_kernel, layers, tuple(names)),
        out_shape=[jax.ShapeDtypeStruct(shape, kind) for _, shape, kind in outs],
        in_specs=in_specs,
        out_specs=[pl.BlockSpec(memory_space=pltpu.VMEM)] * len(outs),
        scratch_shapes=[pltpu.VMEM(shape, kind) for _, shape, kind in scratch]
        + [kind for _, kind in waits],
        compiler_params=pltpu.CompilerParams(
            collective_id=0, has_side_effects=True, vmem_limit_bytes=67043328
        ),
    )(*args)


def per_device_linked(
    layers,
    block_input,
    segment_ids,
    output_grad,
    prenorm_one,
    inproj_one,
    outproj_one,
    midnorm_one,
    expand_one,
    shrink_one,
    prenorm_two,
    inproj_two,
    outproj_two,
    midnorm_two,
    expand_two,
    shrink_two,
):
    width = block_input.shape[1]
    hidden = expand_one.shape[1]
    gains = jnp.stack([prenorm_one, midnorm_one, prenorm_two, midnorm_two], axis=1)
    gain_rows = jnp.pad(gains, ((0, 0), (0, PIECE - 4)))
    weights = (
        inproj_one,
        outproj_one.T,
        expand_one,
        shrink_one.T,
        inproj_two,
        outproj_two.T,
        expand_two,
        shrink_two.T,
    )
    output, grad, total = run_layers(
        layers, block_input, segment_ids, output_grad, gain_rows, weights
    )

    def took(start, size):
        return total[:, start : start + size]

    def weights_of(base, proj):
        return (
            proj,
            took(base, width).T,
            took(base + width, hidden),
            took(base + width + hidden, hidden).T,
        )

    one_grads = weights_of(CHUNK + 3 * width, took(CHUNK, 3 * width))
    base = CHUNK + 4 * width + 2 * hidden
    two_grads = weights_of(
        base + 2 * width, jnp.concatenate([took(base, 2 * width), took(0, width // 2)], axis=1)
    )
    return (
        output,
        grad,
        total[:, PIECE],
        one_grads[0],
        one_grads[1],
        total[:, PIECE + 1],
        one_grads[2],
        one_grads[3],
        total[:, PIECE + 2],
        two_grads[0],
        two_grads[1],
        total[:, PIECE + 3],
        two_grads[2],
        two_grads[3],
    )


def solution(mesh):
    layers = mesh.shape["dp"]
    linked = layers == 4 and mesh.shape["fsdp"] == 8
    step = functools.partial(per_device_linked, layers) if linked else per_device
    return jax.shard_map(
        step,
        mesh=mesh,
        in_specs=(
            P(("dp", "fsdp"), None),
            P(("dp", "fsdp"), None),
            P(("dp", "fsdp"), None),
            P(("dp", "fsdp")),
            P(("dp", "fsdp"), None),
            P(None, ("dp", "fsdp")),
            P(("dp", "fsdp")),
            P(("dp", "fsdp"), None),
            P(None, ("dp", "fsdp")),
            P(("dp", "fsdp")),
            P(("dp", "fsdp"), None),
            P(None, ("dp", "fsdp")),
            P(("dp", "fsdp")),
            P(("dp", "fsdp"), None),
            P(None, ("dp", "fsdp")),
        ),
        out_specs=(
            P(("dp", "fsdp"), None),
            P(("dp", "fsdp"), None),
            P(("dp", "fsdp")),
            P(("dp", "fsdp"), None),
            P(None, ("dp", "fsdp")),
            P(("dp", "fsdp")),
            P(("dp", "fsdp"), None),
            P(None, ("dp", "fsdp")),
            P(("dp", "fsdp")),
            P(("dp", "fsdp"), None),
            P(None, ("dp", "fsdp")),
            P(("dp", "fsdp")),
            P(("dp", "fsdp"), None),
            P(None, ("dp", "fsdp")),
        ),
        check_vma=False,
    )
```
